32 devices in a mesh: axial: 4 (over z), azim: 8 (over y, x, core).
Axes of the slice: x: 2, y: 2, z: 4, core: 2. Of those that a mesh axis runs over, the one named last changes fastest.
Arguments:
- fields: float32 [4096, 4, 1024], P(('axial', 'azim')), may hold values from -6 to 6
- new_owner: int32 [4096, 1], P(('axial', 'azim')), may hold values from 0 to 31; in each aligned block of 128 rows (0 to 127, 128 to 255, ...) at most 6 rows name the same one
- leaflet: bfloat16 [64, 128, 2048], P(None, 'axial', 'azim'), may hold values from -6 to 6
- stiffness: bfloat16 [64, 64], replicated, may hold values from -0.75 to 0.75
- coarse: float32 [2048, 256], P(('axial', 'azim')), may hold values from -6 to 6
- coarse_of_slot: int32 [6144], P(('axial', 'azim')), may hold values from 0 to 63
- viscosity: float32 [4], replicated, may hold values from 0.02 to 0.2
Outputs:
- regridded: float32 [6144, 4, 1024], P(('axial', 'azim'))
The draws below stay inside these ranges and needn't reach their ends.
Inputs may be any that keep to these rules, and one draw needn't show every extreme that they name: `new_owner`: among the patches of one device, at most 6 share a new owner; in some device's patches exactly 6 do.
All inputs are finite; a program needn't handle non-finite values.
Results may differ from the reference program's by a relative error of at most 0.004.
Values may be sent and summed in bfloat16 or wider, within the bound.
A program may use at most 64 MiB of HBM per device.

```python
import math
import jax
import jax.numpy as jnp
import numpy as np
from jax import lax

PR = 16
PC = 64
FIELDS = 4
REC = 64
ZP = 4
CC = 64
STEPS = 2
P_DEV = 128
SC = 6
RS = 192
P_TOTAL = 4096
NA_DEV = 32
NZ_DEV = 256
N_AXIAL = 4
N_AZIM = 8
DEVICES = 32


def plant(values, own_key, low, high):
    extent = values.shape
    index_at = [jax.random.randint(jax.random.fold_in(own_key, axis), (), 0, extent[axis]) for axis in range(len(extent))]
    values = values.at[tuple(index_at)].set(low)
    longest = extent.index(max(extent))
    index_at[longest] = (index_at[longest] + 1) % extent[longest]
    return values.at[tuple(index_at)].set(high)


def block_levels(rng, dims, pieces, smallest, largest):
    def one(dim, parts):
        steps = jax.random.uniform(jax.random.fold_in(jax.random.fold_in(rng, 6), dim), (parts,), jnp.float32, smallest / len(pieces), largest / len(pieces))
        return jnp.repeat(jnp.exp(steps), dims[dim] // parts).reshape((-1,) + (1,) * (len(dims) - dim - 1))

    level = one(*pieces[0])
    for cut in pieces[1:]:
        level = level * one(*cut)
    return level


def routed_block(key, own, number, rows, count, top, most, lean):
    ranking = jax.random.permutation(key, count)
    heavy_load, common = shares(count, rows * top, most, lean, True), shares(count, rows * top, most, lean, False)
    places = jnp.arange(count)

    def named(sizes, turn):
        used = int((sizes > 0).sum())
        fixed = max(1, used // 4)
        passed = fixed + (places - fixed + turn * (used - fixed)) % max(1, count - fixed)
        return jnp.zeros((count,), jnp.int32).at[ranking[jnp.where(places < fixed, places, passed)]].set(jnp.asarray(sizes, jnp.int32))

    sizes = jnp.where(number % 4 == 0, named(heavy_load, number // 4), named(common, number - number // 4 - 1))
    mixed = jax.random.permutation(jax.random.fold_in(own, 3), count)
    giver, taker = mixed[0:count // 2 * 2:2], mixed[1:count // 2 * 2:2]
    margin = jnp.minimum(sizes[giver] - 1, most - sizes[taker]) // 2
    margin = jnp.where((giver == ranking[0]) | (taker == ranking[0]) | (sizes[taker] == 0), 0, jnp.maximum(margin, 0))
    passed = jax.random.randint(jax.random.fold_in(own, 4), (count // 2,), 0, 1 << 20) % (margin + 1)
    sizes = sizes.at[giver].add(-passed).at[taker].add(passed)
    items = jnp.searchsorted(jnp.cumsum(sizes), jnp.arange(rows * top), side="right").astype(jnp.int32)
    table = items.reshape(top, rows).T
    table = table[jax.random.permutation(jax.random.fold_in(own, 1), rows)]
    turn = jax.random.randint(jax.random.fold_in(own, 2), (rows, 1), 0, top)
    return jnp.take_along_axis(table, (jnp.arange(top)[None, :] + turn) % top, axis=1)


def shares(amount, total, most, lean, full):
    weights = [(1 << 20) // math.isqrt(standing ** lean) + 1 for standing in range(1, amount + 1)]
    largest = most if full else min(most, max(-(-total // amount), total * weights[0] // sum(weights)))
    least = 1 if total - largest >= amount - 1 else 0
    given, surplus = [largest] + [least] * (amount - 1), total - largest - least * (amount - 1)
    while surplus > 0:
        free = [i for i in range(1, amount) if given[i] < largest] or [i for i in range(1, amount) if given[i] < most]
        mass, budget = sum([weights[i] for i in free]), surplus
        for i in free:
            more = min(most - given[i], max(1, budget * weights[i] // mass), surplus)
            given[i] = given[i] + more
            surplus = surplus - more
    return np.array(given)


def noise(rng, shape, deviation, reach, cuts=(), kind=jnp.bfloat16):
    loudness = block_levels(rng, shape, cuts, -0.22, 0.18) if cuts else 1.0
    entries = jax.random.normal(rng, shape, jnp.float32) * deviation * loudness
    return jnp.minimum(jnp.maximum(entries, -reach), reach).astype(kind)


def setup_inputs(seed: int = 0) -> dict:
    arg_keys = jax.random.split(jax.random.key(seed), 8)
    fields = noise(arg_keys[0], (P_TOTAL, FIELDS, PR * PC), 1.0, 6.0, ((0, 32),), jnp.float32)
    new_owner_keys = jax.random.split(jax.random.fold_in(arg_keys[1], 1), P_TOTAL // P_DEV)
    new_owner_turns = jax.random.permutation(jax.random.fold_in(arg_keys[1], 3), P_TOTAL // P_DEV)
    new_owner = jax.vmap(lambda own, number: routed_block(jax.random.fold_in(arg_keys[1], 2), own, number, P_DEV, DEVICES, 1, SC, 2))(new_owner_keys, new_owner_turns).reshape((P_TOTAL, 1))
    leaflet = noise(arg_keys[2], (REC, NA_DEV * N_AXIAL, NZ_DEV * N_AZIM), 1.0, 6.0, ((1, 4), (2, 8)))
    stiffness = noise(arg_keys[3], (REC, REC), REC ** -0.5, 0.75)
    coarse = noise(arg_keys[4], (DEVICES * CC, FIELDS * PC), 1.0, 6.0, ((0, 32),), jnp.float32)
    coarse_of_slot = plant(jax.random.randint(arg_keys[5], (DEVICES * RS,), 0, CC), jax.random.fold_in(arg_keys[5], 1), 0, CC - 1).astype(jnp.int32)
    viscosity = jnp.clip(jax.random.uniform(arg_keys[6], (FIELDS,), jnp.float32, 0.02, 0.2), 0.02, 0.2)
    return dict(fields=fields, new_owner=new_owner, leaflet=leaflet, stiffness=stiffness, coarse=coarse, coarse_of_slot=coarse_of_slot, viscosity=viscosity)


SPREAD = 0.25


def interp_table(coarse_cols):
    fine_col = jnp.arange(2 * coarse_cols)
    nearest = fine_col // 2
    second = jnp.where(fine_col % 2 == 0, jnp.maximum(nearest - 1, 0), jnp.minimum(nearest + 1, coarse_cols - 1))
    coarse_row = jnp.arange(coarse_cols)[:, None]
    return 0.75 * (coarse_row == nearest[None, :]).astype(jnp.float32) + 0.25 * (coarse_row == second[None, :]).astype(jnp.float32)


def viscous(state, ghosts, viscosity):
    row_pad = jnp.concatenate([ghosts[:, :, 0:1, :], state, ghosts[:, :, 1:2, :]], axis=2)
    col_pad = jnp.pad(state, ((0, 0), (0, 0), (0, 0), (1, 1)))
    laplace = row_pad[:, :, 2:, :] + row_pad[:, :, :-2, :] + col_pad[:, :, :, 2:] + col_pad[:, :, :, :-2] - 4.0 * state
    return state + viscosity[None, :, None, None] * laplace


def reference(fields, new_owner, leaflet, stiffness, coarse, coarse_of_slot, viscosity):
    points = leaflet.astype(jnp.float32)
    padded = jnp.pad(points, ((0, 0), (1, 1), (0, 0)))
    laplace = padded[:, 2:, :] + padded[:, :-2, :] + jnp.roll(points, 1, 2) + jnp.roll(points, -1, 2) - 4.0 * points
    laplace = laplace.astype(jnp.bfloat16)
    tension = jnp.dot(stiffness, laplace.reshape(REC, -1), preferred_element_type=jnp.float32).astype(jnp.bfloat16)
    tension = tension.reshape(REC, N_AXIAL, NA_DEV, N_AZIM, ZP, PC)
    sheets = tension.transpose(1, 3, 2, 4, 0, 5).reshape(P_TOTAL, FIELDS, PR * PC)
    forced = fields + SPREAD * sheets.astype(jnp.float32)

    owners = new_owner.reshape(DEVICES, P_DEV)
    position = jnp.arange(P_DEV)

    def ranks(owner_row):
        earlier = (owner_row[:, None] == owner_row[None, :]) & (position[None, :] < position[:, None])
        return jnp.sum(earlier.astype(jnp.int32), axis=1)

    ranked = lax.map(ranks, owners)
    target = owners * RS + jnp.arange(DEVICES, dtype=jnp.int32)[:, None] * SC + ranked
    placed = jnp.zeros((DEVICES * RS, FIELDS, PR * PC), jnp.float32).at[target.reshape(-1).astype(jnp.int32)].set(forced)

    interp = interp_table(PC // 2)

    def relax(inputs):
        blocks, strips, picked = inputs
        chosen = jnp.take(strips, picked, axis=0).reshape(RS, FIELDS, 2, PC // 2)
        ghosts = jnp.einsum("sfgk,kc->sfgc", chosen, interp, precision=lax.Precision.HIGHEST)
        state = blocks.reshape(RS, FIELDS, PR, PC)
        for sweep in range(STEPS):
            state = viscous(state, ghosts, viscosity)
        return state.reshape(RS, FIELDS, PR * PC)

    result = lax.map(relax, (placed.reshape(DEVICES, RS, FIELDS, PR * PC), coarse.reshape(DEVICES, CC, FIELDS * PC), coarse_of_slot.reshape(DEVICES, RS)))
    return result.reshape(DEVICES * RS, FIELDS, PR * PC)
```

```python
import functools
import jax
import jax.numpy as jnp
from jax import lax
from jax.experimental import pallas as pl
from jax.experimental.pallas import tpu as pltpu
from jax.sharding import PartitionSpec as P

PC = 64
FIELDS = 4
STEPS = 2
SPREAD = 0.25
LANES = 128
MESH = pl.DeviceIdType.MESH
F32 = jnp.float32
BF16 = jnp.bfloat16


def iota(shape, dim):
    return lax.broadcasted_iota(jnp.int32, shape, dim)


def peer(i, n_ax, n_az):
    j = i // n_az
    da = lax.rem(n_ax // 2 + ((j + 1) // 2) * (1 - 2 * lax.rem(j, 2)), n_ax)
    return da, lax.rem(lax.rem(i, n_az) + 1, n_az)


def send_kernel(
    n_ax, n_az, each, owner_hbm, slot_hbm, nu_hbm, fields_hbm, leaf_hbm, stiff_hbm, coarse_hbm, out_ref,
    owner_ref, slot_ref, nu_ref, fields_ref, leaf_ref, stiff_ref, coarse_ref, load_sem,
    rows_f, cols_f, edge_rows, edge_cols, got_rows, got_cols, lap_ref, forced_ref, packed_ref,
    landed_ref, strip_ref, pick_row, pick_ref,
    halo_send, halo_recv, send_sem, recv_sem, pick_sem, closed_sem,
):
    a = lax.axis_index("axial")
    z = lax.axis_index("azim")
    me = a * n_az + z
    devices = n_ax * n_az
    records, rows, cols = leaf_ref.shape
    patches, height, _ = fields_ref.shape
    blocks = rows // 8

    pairs_in = (
        (leaf_hbm, leaf_ref), (stiff_hbm, stiff_ref), (owner_hbm, owner_ref), (coarse_hbm, coarse_ref),
        (slot_hbm, slot_ref), (nu_hbm, nu_ref), (fields_hbm, fields_ref),
    )
    loads = [
        pltpu.make_async_copy(src, dst, load_sem.at[i]) for i, (src, dst) in enumerate(pairs_in)
    ]
    for load in loads:
        load.start()
    got_rows[...] = jnp.zeros_like(got_rows)
    barrier = pltpu.get_barrier_semaphore()

    row_peers = [(a, lax.rem(z + dz, n_az)) for dz in range(1, n_az)]
    column_peers = [(lax.rem(a + da, n_ax), z) for da in range(1, n_ax)]
    for other in row_peers + column_peers:
        pl.semaphore_signal(barrier, inc=1, device_id=other, device_id_type=MESH)

    row_id = iota((rows, LANES), 0)
    lane_id = iota((rows, LANES), 1)
    eye_low = lane_id == row_id
    eye_high = lane_id == row_id + rows

    def edges(k, carry):
        x = leaf_ref[k].astype(F32)
        rows_f[0, pl.ds(k, 1), :] = x[0:1, :]
        rows_f[1, pl.ds(k, 1), :] = x[rows - 1:rows, :]
        first = jnp.broadcast_to(x[:, 0:1], (rows, LANES))
        last = jnp.broadcast_to(x[:, cols - 1:cols], (rows, LANES))
        both = jnp.where(eye_low, first, jnp.where(eye_high, last, 0.0))
        cols_f[pl.ds(k, 1), :] = jnp.sum(both, axis=0, keepdims=True)
        return carry

    loads[0].wait()
    lax.fori_loop(0, records, edges, 0, unroll=4)
    edge_rows[...] = rows_f[...].astype(BF16)
    edge_cols[...] = cols_f[...].astype(BF16)
    wide_row = iota((rows, cols), 0)
    wide_lane = iota((rows, cols), 1)

    def laplace(k, carry):
        x = leaf_ref[k].astype(F32)
        north = jnp.where(wide_row == 0, 0.0, pltpu.roll(x, 1, 0))
        south = jnp.where(wide_row == rows - 1, 0.0, pltpu.roll(x, rows - 1, 0))
        west = jnp.where(wide_lane == 0, 0.0, pltpu.roll(x, 1, 1))
        east = jnp.where(wide_lane == cols - 1, 0.0, pltpu.roll(x, cols - 1, 1))
        total = south + north + west + east - 4.0 * x
        for b in range(blocks):
            lap_ref[b, pl.ds(pl.multiple_of(k * 8, 8), 8), :] = total[b * 8:(b + 1) * 8, :]
        return carry

    lax.fori_loop(0, records // 2, laplace, 0, unroll=4)
    pl.semaphore_wait(barrier, len(row_peers) + len(column_peers))
    for other in row_peers:
        pl.semaphore_signal(closed_sem, inc=1, device_id=other, device_id_type=MESH)

    def halo(src, dst, i, device):
        return pltpu.make_async_remote_copy(
            src_ref=src, dst_ref=dst, send_sem=halo_send.at[i], recv_sem=halo_recv.at[i],
            device_id=device, device_id_type=MESH,
        )

    down = halo(edge_rows.at[1], got_rows.at[0], 0, (lax.rem(a + 1, n_ax), z))
    up = halo(edge_rows.at[0], got_rows.at[1], 1, (lax.rem(a + n_ax - 1, n_ax), z))
    right = halo(edge_cols, got_cols.at[0], 2, (a, lax.rem(z + 1, n_az)))
    left = halo(edge_cols, got_cols.at[1], 3, (a, lax.rem(z + n_az - 1, n_az)))

    @pl.when(a < n_ax - 1)
    def _():
        down.start()

    @pl.when(a > 0)
    def _():
        up.start()

    right.start()
    left.start()

    lax.fori_loop(records // 2, records, laplace, 0, unroll=4)
    for load in loads[1:6]:
        load.wait()
    pairs = records // FIELDS // 2
    width = pairs * FIELDS
    big = 8 * records
    out_row = iota((big, records), 0)
    record = iota((big, records), 1)
    within = lax.rem(out_row, width)
    wanted = lax.rem(within, FIELDS) * (2 * pairs) + 2 * (within // FIELDS) + out_row // (8 * width)
    row_pick = (record == wanted).astype(BF16)
    col_pick = (iota((records, big), 0) == iota((records, big), 1) // 8).astype(BF16)
    spread = jnp.dot(stiff_ref[...], col_pick, preferred_element_type=F32).astype(BF16)
    spread = jnp.dot(row_pick, spread, preferred_element_type=F32)
    same = lax.rem(iota((big, big), 0) // width, 8) == lax.rem(iota((big, big), 1), 8)
    law = jnp.where(same, spread, 0.0).astype(BF16)
    forced_ref[patches] = jnp.zeros(forced_ref.shape[1:], BF16)
    pick_slots(each, owner_ref, pick_row)
    picked = pltpu.make_async_copy(pick_row, pick_ref, pick_sem)
    picked.start()
    interpolate(coarse_ref, strip_ref)

    @pl.when(a > 0)
    def _():
        down.wait_recv()

    @pl.when(a < n_ax - 1)
    def _():
        up.wait_recv()

    right.wait_recv()
    left.wait_recv()
    rows_f2 = got_rows[...].astype(F32)
    cols_l = got_cols[0].astype(F32)
    cols_r = got_cols[1].astype(F32)

    @pl.when(a < n_ax - 1)
    def _():
        down.wait_send()

    @pl.when(a > 0)
    def _():
        up.wait_send()

    right.wait_send()
    left.wait_send()
    rows_f[...] = rows_f2
    cols_f[...] = jnp.where(iota(cols_l.shape, 1) < rows, cols_r, cols_l)
    first_row = iota((8, cols), 0) == 0
    last_row = iota((8, cols), 0) == 7
    first_lane = lane_id == 0
    last_lane = lane_id == LANES - 1

    def sides(k, carry):
        halo_cols = jnp.broadcast_to(cols_f[pl.ds(k, 1), :], (rows, LANES))
        after = jnp.sum(jnp.where(eye_low, halo_cols, 0.0), axis=1, keepdims=True)
        before = jnp.sum(jnp.where(eye_high, halo_cols, 0.0), axis=1, keepdims=True)
        west = jnp.where(first_lane, before, 0.0)
        east = jnp.where(last_lane, after, 0.0)
        here = pl.ds(pl.multiple_of(k * 8, 8), 8)
        lap_ref[0, here, :] += jnp.where(first_row, rows_f[0, pl.ds(k, 1), :], 0.0)
        lap_ref[blocks - 1, here, :] += jnp.where(last_row, rows_f[1, pl.ds(k, 1), :], 0.0)
        for b in range(blocks):
            lap_ref[b, here, :LANES] += west[b * 8:(b + 1) * 8]
            lap_ref[b, here, cols - LANES:] += east[b * 8:(b + 1) * 8]
        return carry

    lax.fori_loop(0, records, sides, 0, unroll=8)
    loads[6].wait()
    low = iota((width, LANES), 1) < PC
    across = cols // PC

    def force(b, carry):
        tension = jnp.dot(law, lap_ref[b].astype(BF16), preferred_element_type=F32)
        tension = tension.astype(BF16).astype(F32) * SPREAD
        for r in range(8):
            for t in range(cols // LANES):
                even = tension[r * width:(r + 1) * width, t * LANES:(t + 1) * LANES]
                odd = tension[(8 + r) * width:(9 + r) * width, t * LANES:(t + 1) * LANES]
                p = (b * 8 + r) * across + 2 * t
                first = jnp.where(low, even, pltpu.roll(odd, PC, 1))
                second = jnp.where(low, pltpu.roll(even, PC, 1), odd)
                forced_ref[p] = (fields_ref[p] + first).astype(BF16)
                forced_ref[p + 1] = (fields_ref[p + 1] + second).astype(BF16)
        return carry

    lax.fori_loop(0, blocks, force, 0)

    picked.wait()
    pl.semaphore_wait(closed_sem, len(row_peers))

    def outgoing(i):
        da, dz = peer(i, n_ax, n_az)
        ta, tz = lax.rem(a + da, n_ax), lax.rem(z + dz, n_az)
        other = ta * n_az + tz
        return other, pltpu.make_async_remote_copy(
            src_ref=packed_ref.at[other], dst_ref=landed_ref.at[me],
            send_sem=send_sem.at[i], recv_sem=recv_sem.at[i],
            device_id=(ta, tz), device_id_type=MESH,
        )

    def send(i, carry):
        other, copy = outgoing(i)
        for k in range(each):
            packed_ref[other, k] = forced_ref[pick_ref[0, other * each + k]]
        copy.start()
        return carry

    lax.fori_loop(0, devices - 1, send, 0)

    row = iota((height, LANES), 0)
    nu = jnp.full((height, LANES), nu_ref[0], F32)
    for f in range(1, FIELDS):
        nu = jnp.where(lax.rem(row, FIELDS) == f, nu_ref[f], nu)

    for k in range(each):
        ghost = strip_ref[slot_ref[me * each + k]]
        block = forced_ref[pick_ref[0, me * each + k]].astype(F32)
        out_ref[me, k] = relax(block, ghost, nu)

    def arrive(turn, carry):
        i = lax.rem(turn + devices - n_az, devices - 1)
        da, dz = peer(i, n_ax, n_az)
        source = lax.rem(a + n_ax - da, n_ax) * n_az + lax.rem(z + n_az - dz, n_az)
        pltpu.make_async_remote_copy(
            src_ref=packed_ref.at[source], dst_ref=landed_ref.at[source],
            send_sem=send_sem.at[i], recv_sem=recv_sem.at[i],
            device_id=(a, z), device_id_type=MESH,
        ).wait_recv()
        for k in range(each):
            ghost = strip_ref[slot_ref[source * each + k]]
            out_ref[source, k] = relax(landed_ref[source, k].astype(F32), ghost, nu)
        return carry

    lax.fori_loop(0, devices - 1, arrive, 0)

    def finish(i, carry):
        outgoing(i)[1].wait_send()
        return carry

    lax.fori_loop(0, devices - 1, finish, 0)


def pick_slots(each, owner_ref, pick_row):
    patches = owner_ref.shape[1]
    slots = pick_row.shape[1]
    square = (patches, patches)
    eye = iota(square, 0) == iota(square, 1)
    owner = owner_ref[...]
    across = jnp.broadcast_to(owner, square)
    along = jnp.sum(jnp.where(eye, across, 0), axis=1, keepdims=True)
    earlier = (along == across) & (iota(square, 0) < iota(square, 1))
    rank = jnp.sum(earlier.astype(jnp.int32), axis=0, keepdims=True)
    target = jnp.broadcast_to(owner * each + rank, square)
    target = jnp.sum(jnp.where(eye, target, 0), axis=1, keepdims=True)
    shape = (patches, slots)
    taken = target == iota(shape, 1)
    pick_row[...] = patches + jnp.sum(
        jnp.where(taken, iota(shape, 0) - patches, 0), axis=0, keepdims=True
    )


def interpolate(coarse_ref, strip_ref):
    fine = iota((PC, LANES), 1)
    src = iota((PC, LANES), 0)
    cell = lax.rem(fine, PC)
    near = (fine // PC) * (PC // 2) + cell // 2
    second = jnp.where(
        lax.rem(fine, 2) == 0,
        jnp.where(cell == 0, near, near - 1),
        jnp.where(cell == PC - 1, near, near + 1),
    )
    table = (0.75 * (src == near).astype(F32) + 0.25 * (src == second).astype(F32)).astype(BF16)
    for f in range(FIELDS):
        raw = coarse_ref[:, f * PC:(f + 1) * PC]
        top = raw.astype(BF16)
        rest = (raw - top.astype(F32)).astype(BF16)
        fine_cells = jnp.dot(top, table, preferred_element_type=F32)
        fine_cells = fine_cells + jnp.dot(rest, table, preferred_element_type=F32)
        strip_ref[:, f, :] = fine_cells
        strip_ref[:, FIELDS + f, :] = fine_cells


def relax(state, ghost, nu):
    shape = (8, LANES)
    lane = iota(shape, 1)
    low = iota(shape, 0) < FIELDS
    cell = lax.rem(lane, PC)
    up = (lane < PC) & low
    down = (lane >= PC) & (iota(shape, 0) >= FIELDS)
    count = state.shape[0] // 8
    tiles = [state[8 * j:8 * j + 8] for j in range(count)]
    for _ in range(STEPS):
        swap = [pltpu.roll(t, PC, 1) for t in tiles]
        turned = [ghost] + [pltpu.roll(t, FIELDS, 0) for t in swap] + [ghost]
        fresh = []
        for j, t in enumerate(tiles):
            beyond = jnp.where(up, turned[j], jnp.where(down, turned[j + 2], turned[j + 1]))
            west = jnp.where(cell == 0, 0.0, pltpu.roll(t, 1, 1))
            east = jnp.where(cell == PC - 1, 0.0, pltpu.roll(t, LANES - 1, 1))
            total = swap[j] + beyond + west + east - 4.0 * t
            fresh.append(t + nu[8 * j:8 * j + 8] * total)
        tiles = fresh
    return jnp.concatenate(tiles, axis=0)


def shards(mesh, fields, new_owner, leaflet, stiffness, coarse, coarse_of_slot, viscosity):
    n_ax, n_az = mesh.shape["axial"], mesh.shape["azim"]
    devices = n_ax * n_az
    patches, _, section = fields.shape
    records, rows, cols = leaflet.shape
    each = max(2, 3 * patches // (2 * devices))
    slots = devices * each
    wide = -(-slots // LANES) * LANES
    height = FIELDS * section // LANES
    view = fields.reshape(patches, FIELDS, section // LANES, LANES).transpose(0, 2, 1, 3)
    view = view.reshape(patches, height, LANES)
    given = (new_owner.reshape(1, patches), coarse_of_slot, viscosity, view, leaflet, stiffness, coarse)
    out = pl.pallas_call(
        functools.partial(send_kernel, n_ax, n_az, each),
        out_shape=pltpu.VMEM((devices, each, height, LANES), F32),
        in_specs=[pl.BlockSpec(memory_space=pltpu.HBM)] * 7,
        out_specs=pl.BlockSpec(memory_space=pltpu.VMEM),
        scratch_shapes=[
            pltpu.VMEM((1, patches), jnp.int32),
            pltpu.SMEM((slots,), jnp.int32),
            pltpu.SMEM((FIELDS,), F32),
            pltpu.VMEM((patches, height, LANES), F32),
            pltpu.VMEM(leaflet.shape, BF16),
            pltpu.VMEM(stiffness.shape, BF16),
            pltpu.VMEM(coarse.shape, F32),
            pltpu.SemaphoreType.DMA((7,)),
            pltpu.VMEM((2, records, cols), F32),
            pltpu.VMEM((records, LANES), F32),
            pltpu.VMEM((2, records, cols), BF16),
            pltpu.VMEM((records, LANES), BF16),
            pltpu.VMEM((2, records, cols), BF16),
            pltpu.VMEM((2, records, LANES), BF16),
            pltpu.VMEM((rows // 8, 8 * records, cols), F32),
            pltpu.VMEM((patches + 1, height, LANES), BF16),
            pltpu.VMEM((devices, each, height, LANES), BF16),
            pltpu.VMEM((devices, each, height, LANES), BF16),
            pltpu.VMEM((coarse.shape[0], 2 * FIELDS, LANES), F32),
            pltpu.VMEM((1, wide), jnp.int32),
            pltpu.SMEM((1, wide), jnp.int32),
            pltpu.SemaphoreType.DMA((4,)),
            pltpu.SemaphoreType.DMA((4,)),
            pltpu.SemaphoreType.DMA((devices - 1,)),
            pltpu.SemaphoreType.DMA((devices - 1,)),
            pltpu.SemaphoreType.DMA,
            pltpu.SemaphoreType.REGULAR,
        ],
        compiler_params=pltpu.CompilerParams(
            collective_id=0, has_side_effects=True, vmem_limit_bytes=40 << 20
        ),
        name="regrid",
    )(*[pltpu.with_memory_space_constraint(v, pltpu.HBM) for v in given])
    out = out.reshape(slots, section // LANES, FIELDS, LANES).transpose(0, 2, 1, 3)
    return out.reshape(slots, FIELDS, section)


def solution(mesh):
    placed = (
        P(("axial", "azim"), None, None),
        P(("axial", "azim"), None),
        P(None, "axial", "azim"),
        P(),
        P(("axial", "azim"), None),
        P(("axial", "azim")),
        P(),
    )
    return jax.shard_map(
        functools.partial(shards, mesh),
        mesh=mesh,
        in_specs=placed,
        out_specs=P(("axial", "azim"), None, None),
        check_vma=False,
    )
```

```python
import functools
import jax
import jax.numpy as jnp
from jax import lax
from jax.experimental import pallas as pl
from jax.experimental.pallas import tpu as pltpu
from jax.sharding import PartitionSpec as P

PC = 64
FIELDS = 4
STEPS = 2
SPREAD = 0.25
PHASES = 2
BAND = 16
TOGETHER = 4
LANES = 128
MESH = pl.DeviceIdType.MESH
F32 = jnp.float32
BF16 = jnp.bfloat16


def iota(shape, dim):
    return lax.broadcasted_iota(jnp.int32, shape, dim)


def shifts(n_ax):
    if n_ax & (n_ax - 1):
        away = [n_ax // 2 + ((j + 1) // 2) * (1 - 2 * (j % 2)) for j in range(n_ax)]
        return [d % n_ax for d in away]
    return [k ^ (k >> 1) for k in reversed(range(n_ax))]


def partner(a, shift, n_ax, back=False):
    if n_ax & (n_ax - 1):
        return lax.rem(a + (n_ax - shift if back else shift), n_ax)
    return a ^ shift


def send_kernel(
    n_ax, n_az, each, owner_hbm, slot_hbm, nu_hbm, fields_hbm, leaf_hbm, stiff_hbm, coarse_hbm, out_ref,
    owner_ref, slot_ref, nu_ref, fields_ref, leaf_ref, stiff_ref, coarse_ref, load_sem,
    edge_rows, edge_cols, got_rows, got_cols, law_ref, side_ref, coupled_ref, forced_ref, packed_ref,
    landed_ref, strip_ref, pick_row, pick_ref,
    halo_send, halo_recv, send_sem, recv_sem, pick_sem, closed_sem,
):
    a = lax.axis_index("axial")
    z = lax.axis_index("azim")
    me = a * n_az + z
    devices = n_ax * n_az
    records, rows, cols = leaf_ref.shape
    patches, height, _ = fields_ref.shape
    blocks = rows // BAND
    deep = records * BAND
    pairs = records // FIELDS // 2
    share = pairs // PHASES * FIELDS
    wide = 2 * share

    pairs_in = (
        (owner_hbm, owner_ref), (stiff_hbm, stiff_ref), (leaf_hbm, leaf_ref), (fields_hbm, fields_ref),
        (coarse_hbm, coarse_ref), (slot_hbm, slot_ref), (nu_hbm, nu_ref),
    )
    loads = [
        pltpu.make_async_copy(src, dst, load_sem.at[i]) for i, (src, dst) in enumerate(pairs_in)
    ]
    for load in loads:
        load.start()
    got_rows[...] = jnp.zeros_like(got_rows)
    barrier = pltpu.get_barrier_semaphore()

    row_peers = [(a, lax.rem(z + dz, n_az)) for dz in range(1, n_az)]
    column_peers = [(lax.rem(a + da, n_ax), z) for da in range(1, n_ax)]
    for other in row_peers + column_peers:
        pl.semaphore_signal(barrier, inc=1, device_id=other, device_id_type=MESH)

    column = iota((records, deep), 1)
    belongs = iota((records, deep), 0) == column // BAND
    gather = belongs.astype(BF16)
    gather_first = (belongs & (lax.rem(column, BAND) == 0)).astype(BF16)
    gather_last = (belongs & (lax.rem(column, BAND) == BAND - 1)).astype(BF16)
    source = iota((cols, LANES), 0)
    odd_lane = lax.rem(iota((cols, LANES), 1), 2) == 1
    ends = (((source == cols - 1) & ~odd_lane) | ((source == 0) & odd_lane)).astype(BF16)

    loads[0].wait()
    pick_slots(each, owner_ref, pick_row)
    picked = pltpu.make_async_copy(pick_row, pick_ref, pick_sem)
    picked.start()
    forced_ref[patches] = jnp.zeros(forced_ref.shape[1:], BF16)

    loads[1].wait()
    spread = jnp.dot(stiff_ref[...], gather, preferred_element_type=F32).astype(BF16)
    row_of = lax.rem(iota((wide, deep), 1), BAND)
    small = []
    for h in range(PHASES):
        order = iota((wide, records), 0)
        within = lax.rem(order, share)
        wanted = lax.rem(within, FIELDS) * (2 * pairs) + order // share
        wanted = wanted + 2 * (h * (pairs // PHASES) + within // FIELDS)
        chosen = (iota((wide, records), 1) == wanted).astype(BF16)
        small.append(jnp.dot(chosen, stiff_ref[...], preferred_element_type=F32).astype(BF16))
        base = jnp.dot(chosen, spread, preferred_element_type=F32)

        def fill(r, carry, h=h, base=base):
            here = pl.ds(pl.multiple_of(r * wide, wide), wide)
            law_ref[h, here, :] = jnp.where(row_of == r, base, 0.0).astype(BF16)
            return carry

        lax.fori_loop(0, BAND, fill, 0, unroll=2)

    loads[2].wait()
    band_lane = iota((BAND, LANES), 1)
    band_row = iota((BAND, LANES), 0)

    def band(b):
        return leaf_ref[:, pl.ds(pl.multiple_of(b * BAND, BAND), BAND), :].reshape(deep, cols)

    total = jnp.zeros((records, LANES), F32)
    for b in range(blocks):
        both = jnp.dot(band(b), ends, preferred_element_type=F32).reshape(records, BAND, LANES)
        twice = 2 * (band_row + b * BAND)
        kept = (band_lane == twice) | (band_lane == lax.rem(twice + LANES - 1, LANES))
        both = jnp.where(kept[None], both, 0.0).astype(BF16).reshape(deep, LANES)
        total = total + jnp.dot(gather, both, preferred_element_type=F32)
    edge_cols[...] = total.astype(BF16)
    edge_rows[0] = jnp.dot(gather_first, band(0), preferred_element_type=F32).astype(BF16)
    edge_rows[1] = jnp.dot(gather_last, band(blocks - 1), preferred_element_type=F32).astype(BF16)

    pl.semaphore_wait(barrier, len(row_peers) + len(column_peers))
    for other in row_peers:
        pl.semaphore_signal(closed_sem, inc=1, device_id=other, device_id_type=MESH)

    def halo(src, dst, i, device):
        return pltpu.make_async_remote_copy(
            src_ref=src, dst_ref=dst, send_sem=halo_send.at[i], recv_sem=halo_recv.at[i],
            device_id=device, device_id_type=MESH,
        )

    down = halo(edge_rows.at[1], got_rows.at[0], 0, (lax.rem(a + 1, n_ax), z))
    up = halo(edge_rows.at[0], got_rows.at[1], 1, (lax.rem(a + n_ax - 1, n_ax), z))
    right = halo(edge_cols, got_cols.at[0], 2, (a, lax.rem(z + 1, n_az)))
    left = halo(edge_cols, got_cols.at[1], 3, (a, lax.rem(z + n_az - 1, n_az)))

    @pl.when(a < n_ax - 1)
    def _():
        down.start()

    @pl.when(a > 0)
    def _():
        up.start()

    right.start()
    left.start()

    def couple(h):
        def one(b, carry):
            found = jnp.dot(law_ref[h], band(b), preferred_element_type=F32)
            coupled_ref[h, pl.ds(1 + b * BAND, BAND)] = found.reshape(BAND, wide, cols)
            return carry

        lax.fori_loop(0, blocks, one, 0)

    couple(0)

    @pl.when(a > 0)
    def _():
        down.wait_recv()

    @pl.when(a < n_ax - 1)
    def _():
        up.wait_recv()

    right.wait_recv()
    left.wait_recv()
    even = lax.rem(iota((records, LANES), 1), 2) == 0
    beside = jnp.where(even, got_cols[0].astype(F32), got_cols[1].astype(F32)).astype(BF16)

    def border(h):
        side_ref[h] = jnp.dot(small[h], beside, preferred_element_type=F32)
        coupled_ref[h, 0] = jnp.dot(small[h], got_rows[0], preferred_element_type=F32)
        coupled_ref[h, rows + 1] = jnp.dot(small[h], got_rows[1], preferred_element_type=F32)

    border(0)

    lane = iota((wide, LANES), 1)
    first_lane = lane == 0
    last_lane = lane == LANES - 1
    low = iota((share, LANES), 1) < PC
    across = cols // PC
    tiles = cols // LANES

    def force(h):
        part = slice(h * share, (h + 1) * share)

        def some(turn, carry):
            stored = []
            for r in [turn * TOGETHER + n for n in range(TOGETHER)]:
                beyond = pltpu.roll(side_ref[h], lax.rem(2 * LANES - 2 * r, LANES), 1)
                here = [coupled_ref[h, r + 1, :, t * LANES:(t + 1) * LANES] for t in range(tiles)]
                west = [pltpu.roll(v, 1, 1) for v in here]
                east = [pltpu.roll(v, LANES - 1, 1) for v in here]
                for t in range(tiles):
                    cut = slice(t * LANES, (t + 1) * LANES)
                    before = west[t - 1] if t else beyond
                    after = east[t + 1] if t < tiles - 1 else beyond
                    sums = jnp.where(first_lane, before, west[t]) + jnp.where(last_lane, after, east[t])
                    sums = sums + (coupled_ref[h, r, :, cut] + coupled_ref[h, r + 2, :, cut])
                    change = SPREAD * sums - (4.0 * SPREAD) * here[t]
                    top, bottom = change[:share], change[share:]
                    turned = pltpu.roll(jnp.where(low, bottom, top), PC, 1)
                    p = r * across + 2 * t
                    stored.append((p, (fields_ref[p, part] + jnp.where(low, top, turned)).astype(BF16)))
                    stored.append((p + 1, (fields_ref[p + 1, part] + jnp.where(low, turned, bottom)).astype(BF16)))
            for p, value in stored:
                forced_ref[p, part] = value
            return carry

        lax.fori_loop(0, rows // TOGETHER, some, 0)

    order = shifts(n_ax)
    turns = [n_az - (shift == 0) for shift in order]

    def piece(ref, at, h):
        return ref.at[at] if h is None else ref.at[at, :, h * share:(h + 1) * share]

    def outgoing(j, d, h=None):
        ta, tz = partner(a, order[j], n_ax), lax.rem(z + d + 1, n_az)
        other = ta * n_az + tz
        return other, pltpu.make_async_remote_copy(
            src_ref=piece(packed_ref, other, h), dst_ref=piece(landed_ref, me, h),
            send_sem=send_sem.at[h or 0, j * n_az + d], recv_sem=recv_sem.at[h or 0, j * n_az + d],
            device_id=(ta, tz), device_id_type=MESH,
        )

    def incoming(j, d, h=None):
        source = partner(a, order[j], n_ax, back=True) * n_az + lax.rem(z + n_az - d - 1, n_az)
        return source, pltpu.make_async_remote_copy(
            src_ref=piece(packed_ref, source, h), dst_ref=piece(landed_ref, source, h),
            send_sem=send_sem.at[h or 0, j * n_az + d], recv_sem=recv_sem.at[h or 0, j * n_az + d],
            device_id=(a, z), device_id_type=MESH,
        )

    def send_all(j, h=None):
        part = slice(None) if h is None else slice(h * share, (h + 1) * share)

        def send(d, carry):
            other, copy = outgoing(j, d, h)
            for k in range(each):
                packed_ref[other, k, part] = forced_ref[pick_ref[0, other * each + k], part]
            copy.start()
            return carry

        lax.fori_loop(0, turns[j], send, 0)

    halves = [range(PHASES) if j == 0 else (None,) for j in range(n_ax)]

    loads[3].wait()
    force(0)
    picked.wait()
    pl.semaphore_wait(closed_sem, len(row_peers))
    send_all(0, 0)
    for h in range(1, PHASES):
        couple(h)
        border(h)
        force(h)
        send_all(0, h)
    for j in range(1, n_ax):
        send_all(j)

    for load in loads[4:]:
        load.wait()
    interpolate(coarse_ref, strip_ref)
    row = iota((height, LANES), 0)
    nu = jnp.full((height, LANES), nu_ref[0], F32)
    for f in range(1, FIELDS):
        nu = jnp.where(lax.rem(row, FIELDS) == f, nu_ref[f], nu)

    for k in range(each):
        ghost = strip_ref[slot_ref[me * each + k]]
        block = forced_ref[pick_ref[0, me * each + k]].astype(F32)
        out_ref[me, k] = relax(block, ghost, nu)

    def arrive(j, d):
        for h in halves[j]:
            source, copy = incoming(j, d, h)
            copy.wait_recv()
        for k in range(each):
            ghost = strip_ref[slot_ref[source * each + k]]
            out_ref[source, k] = relax(landed_ref[source, k].astype(F32), ghost, nu)

    far = n_ax // 2
    for j in sorted(range(n_ax), key=lambda j: (order[j] > 0, order[j] != far, order[j] > far, -order[j])):
        def one(d, carry, j=j):
            arrive(j, d)
            return carry

        lax.fori_loop(0, turns[j], one, 0)

    for j in range(n_ax):
        def finish(d, carry, j=j):
            for h in halves[j]:
                outgoing(j, d, h)[1].wait_send()
            return carry

        lax.fori_loop(0, turns[j], finish, 0)

    @pl.when(a < n_ax - 1)
    def _():
        down.wait_send()

    @pl.when(a > 0)
    def _():
        up.wait_send()

    right.wait_send()
    left.wait_send()


def pick_slots(each, owner_ref, pick_row):
    patches = owner_ref.shape[1]
    slots = pick_row.shape[1]
    square = (patches, patches)
    eye = iota(square, 0) == iota(square, 1)
    owner = owner_ref[...]
    across = jnp.broadcast_to(owner, square)
    along = jnp.sum(jnp.where(eye, across, 0), axis=1, keepdims=True)
    earlier = (along == across) & (iota(square, 0) < iota(square, 1))
    rank = jnp.sum(earlier.astype(jnp.int32), axis=0, keepdims=True)
    target = jnp.broadcast_to(owner * each + rank, square)
    target = jnp.sum(jnp.where(eye, target, 0), axis=1, keepdims=True)
    shape = (patches, slots)
    taken = target == iota(shape, 1)
    pick_row[...] = patches + jnp.sum(
        jnp.where(taken, iota(shape, 0) - patches, 0), axis=0, keepdims=True
    )


def interpolate(coarse_ref, strip_ref):
    fine = iota((PC, LANES), 1)
    src = iota((PC, LANES), 0)
    cell = lax.rem(fine, PC)
    near = (fine // PC) * (PC // 2) + cell // 2
    second = jnp.where(
        lax.rem(fine, 2) == 0,
        jnp.where(cell == 0, near, near - 1),
        jnp.where(cell == PC - 1, near, near + 1),
    )
    table = (0.75 * (src == near).astype(F32) + 0.25 * (src == second).astype(F32)).astype(BF16)
    for f in range(FIELDS):
        raw = coarse_ref[:, f * PC:(f + 1) * PC]
        top = raw.astype(BF16)
        rest = (raw - top.astype(F32)).astype(BF16)
        fine_cells = jnp.dot(top, table, preferred_element_type=F32)
        fine_cells = fine_cells + jnp.dot(rest, table, preferred_element_type=F32)
        strip_ref[:, f, :] = fine_cells
        strip_ref[:, FIELDS + f, :] = fine_cells


def relax(state, ghost, nu):
    shape = (8, LANES)
    lane = iota(shape, 1)
    low = iota(shape, 0) < FIELDS
    cell = lax.rem(lane, PC)
    up = (lane < PC) & low
    down = (lane >= PC) & (iota(shape, 0) >= FIELDS)
    count = state.shape[0] // 8
    tiles = [state[8 * j:8 * j + 8] for j in range(count)]
    for _ in range(STEPS):
        swap = [pltpu.roll(t, PC, 1) for t in tiles]
        turned = [ghost] + [pltpu.roll(t, FIELDS, 0) for t in swap] + [ghost]
        fresh = []
        for j, t in enumerate(tiles):
            beyond = jnp.where(up, turned[j], jnp.where(down, turned[j + 2], turned[j + 1]))
            west = jnp.where(cell == 0, 0.0, pltpu.roll(t, 1, 1))
            east = jnp.where(cell == PC - 1, 0.0, pltpu.roll(t, LANES - 1, 1))
            total = swap[j] + beyond + west + east - 4.0 * t
            fresh.append(t + nu[8 * j:8 * j + 8] * total)
        tiles = fresh
    return jnp.concatenate(tiles, axis=0)


def shards(mesh, fields, new_owner, leaflet, stiffness, coarse, coarse_of_slot, viscosity):
    n_ax, n_az = mesh.shape["axial"], mesh.shape["azim"]
    devices = n_ax * n_az
    patches, _, section = fields.shape
    records, rows, cols = leaflet.shape
    each = max(2, 3 * patches // (2 * devices))
    slots = devices * each
    wide = -(-slots // LANES) * LANES
    height = FIELDS * section // LANES
    part = records // PHASES
    view = fields.reshape(patches, FIELDS, section // LANES, LANES).transpose(0, 2, 1, 3)
    view = view.reshape(patches, height, LANES)
    given = (new_owner.reshape(1, patches), coarse_of_slot, viscosity, view, leaflet, stiffness, coarse)
    out = pl.pallas_call(
        functools.partial(send_kernel, n_ax, n_az, each),
        out_shape=pltpu.VMEM((devices, each, height, LANES), F32),
        in_specs=[pl.BlockSpec(memory_space=pltpu.HBM)] * 7,
        out_specs=pl.BlockSpec(memory_space=pltpu.VMEM),
        scratch_shapes=[
            pltpu.VMEM((1, patches), jnp.int32),
            pltpu.SMEM((slots,), jnp.int32),
            pltpu.SMEM((FIELDS,), F32),
            pltpu.VMEM((patches, height, LANES), F32),
            pltpu.VMEM(leaflet.shape, BF16),
            pltpu.VMEM(stiffness.shape, BF16),
            pltpu.VMEM(coarse.shape, F32),
            pltpu.SemaphoreType.DMA((7,)),
            pltpu.VMEM((2, records, cols), BF16),
            pltpu.VMEM((records, LANES), BF16),
            pltpu.VMEM((2, records, cols), BF16),
            pltpu.VMEM((2, records, LANES), BF16),
            pltpu.VMEM((PHASES, BAND * part, BAND * records), BF16),
            pltpu.VMEM((PHASES, part, LANES), F32),
            pltpu.VMEM((PHASES, rows + 2, part, cols), F32),
            pltpu.VMEM((patches + 1, height, LANES), BF16),
            pltpu.VMEM((devices, each, height, LANES), BF16),
            pltpu.VMEM((devices, each, height, LANES), BF16),
            pltpu.VMEM((coarse.shape[0], 2 * FIELDS, LANES), F32),
            pltpu.VMEM((1, wide), jnp.int32),
            pltpu.SMEM((1, wide), jnp.int32),
            pltpu.SemaphoreType.DMA((4,)),
            pltpu.SemaphoreType.DMA((4,)),
            pltpu.SemaphoreType.DMA((PHASES, devices)),
            pltpu.SemaphoreType.DMA((PHASES, devices)),
            pltpu.SemaphoreType.DMA,
            pltpu.SemaphoreType.REGULAR,
        ],
        compiler_params=pltpu.CompilerParams(
            collective_id=0, has_side_effects=True, vmem_limit_bytes=40 << 20
        ),
        name="regrid",
    )(*[pltpu.with_memory_space_constraint(v, pltpu.HBM) for v in given])
    out = out.reshape(slots, section // LANES, FIELDS, LANES).transpose(0, 2, 1, 3)
    return out.reshape(slots, FIELDS, section)


def solution(mesh):
    placed = (
        P(("axial", "azim"), None, None),
        P(("axial", "azim"), None),
        P(None, "axial", "azim"),
        P(),
        P(("axial", "azim"), None),
        P(("axial", "azim")),
        P(),
    )
    return jax.shard_map(
        functools.partial(shards, mesh),
        mesh=mesh,
        in_specs=placed,
        out_specs=P(("axial", "azim"), None, None),
        check_vma=False,
    )
```

```python
import functools
import jax
import jax.numpy as jnp
from jax import lax
from jax.experimental import pallas as pl
from jax.experimental.pallas import tpu as pltpu
from jax.sharding import PartitionSpec as P

PC = 64
FIELDS = 4
STEPS = 2
SPREAD = 0.25
PHASES = 2
BAND = 16
TOGETHER = 4
LANES = 128
MESH = pl.DeviceIdType.MESH
F32 = jnp.float32
BF16 = jnp.bfloat16


def iota(shape, dim):
    return lax.broadcasted_iota(jnp.int32, shape, dim)


def shifts(n_ax):
    if n_ax & (n_ax - 1):
        away = [n_ax // 2 + ((j + 1) // 2) * (1 - 2 * (j % 2)) for j in range(n_ax)]
        return [d % n_ax for d in away]
    return [k ^ (k >> 1) for k in reversed(range(n_ax))]


def partner(a, shift, n_ax, back=False):
    if n_ax & (n_ax - 1):
        return lax.rem(a + (n_ax - shift if back else shift), n_ax)
    return a ^ shift


def send_kernel(
    n_ax, n_az, each, owner_hbm, slot_hbm, nu_hbm, fields_hbm, leaf_hbm, stiff_hbm, coarse_hbm, out_ref,
    owner_ref, slot_ref, nu_ref, fields_ref, leaf_ref, stiff_ref, coarse_ref, load_sem,
    edge_rows, edge_cols, got_rows, got_cols, lap_ref, law_ref, side_ref, coupled_ref, forced_ref, packed_ref,
    landed_ref, strip_ref, pick_row, pick_ref,
    halo_send, halo_recv, send_sem, recv_sem, pick_sem, chain_sem,
):
    a = lax.axis_index("axial")
    z = lax.axis_index("azim")
    me = a * n_az + z
    devices = n_ax * n_az
    records, rows, cols = leaf_ref.shape
    patches, height, _ = fields_ref.shape
    blocks = rows // BAND
    deep = records * BAND
    pairs = records // FIELDS // 2
    share = pairs // PHASES * FIELDS
    wide = 2 * share

    pairs_in = (
        (leaf_hbm, leaf_ref), (owner_hbm, owner_ref), (stiff_hbm, stiff_ref), (fields_hbm, fields_ref),
        (coarse_hbm, coarse_ref), (slot_hbm, slot_ref), (nu_hbm, nu_ref),
    )
    loads = [
        pltpu.make_async_copy(src, dst, load_sem.at[i]) for i, (src, dst) in enumerate(pairs_in)
    ]
    for load in loads:
        load.start()
    got_rows[...] = jnp.zeros_like(got_rows)
    barrier = pltpu.get_barrier_semaphore()

    row_peers = [(a, lax.rem(z + dz, n_az)) for dz in range(1, n_az)]
    for other in row_peers:
        pl.semaphore_signal(barrier, inc=1, device_id=other, device_id_type=MESH)

    above, below = (a + 1, z), (a - 1, z)
    has_above, has_below = a < n_ax - 1, a > 0

    @pl.when(has_above)
    def _():
        pl.semaphore_signal(barrier, inc=1, device_id=above, device_id_type=MESH)

    @pl.when(has_below)
    def _():
        pl.semaphore_signal(barrier, inc=1, device_id=below, device_id_type=MESH)

    column = iota((records, deep), 1)
    belongs = iota((records, deep), 0) == column // BAND
    gather = belongs.astype(BF16)
    gather_first = (belongs & (lax.rem(column, BAND) == 0)).astype(BF16)
    gather_last = (belongs & (lax.rem(column, BAND) == BAND - 1)).astype(BF16)
    source = iota((cols, LANES), 0)
    odd_lane = lax.rem(iota((cols, LANES), 1), 2) == 1
    ends = (((source == cols - 1) & ~odd_lane) | ((source == 0) & odd_lane)).astype(BF16)

    here_col, there_col = iota((cols, cols), 0), iota((cols, cols), 1)
    along = (jnp.abs(here_col - there_col) == 1).astype(F32)
    along = jnp.where(here_col == there_col, -4.0, along).astype(BF16)
    side = 2 * LANES
    here_row, there_row = iota((side, side), 0), iota((side, side), 1)
    upright = (here_row // BAND == there_row // BAND) & (jnp.abs(here_row - there_row) == 1)
    upright = upright.astype(BF16)

    loads[1].wait()
    pick_slots(each, owner_ref, pick_row)
    picked = pltpu.make_async_copy(pick_row, pick_ref, pick_sem)
    picked.start()
    forced_ref[patches] = jnp.zeros(forced_ref.shape[1:], BF16)

    loads[2].wait()
    spread = jnp.dot(stiff_ref[...], gather, preferred_element_type=F32).astype(BF16)
    row_of = lax.rem(iota((wide, deep), 1), BAND)
    small = []
    for h in range(PHASES):
        order = iota((wide, records), 0)
        within = lax.rem(order, share)
        wanted = lax.rem(within, FIELDS) * (2 * pairs) + order // share
        wanted = wanted + 2 * (h * (pairs // PHASES) + within // FIELDS)
        chosen = (iota((wide, records), 1) == wanted).astype(BF16)
        small.append(jnp.dot(chosen, stiff_ref[...], preferred_element_type=F32).astype(BF16))
        base = jnp.dot(chosen, spread, preferred_element_type=F32)

        def fill(r, carry, h=h, base=base):
            here = pl.ds(pl.multiple_of(r * wide, wide), wide)
            law_ref[h, here, :] = jnp.where(row_of == r, base, 0.0).astype(BF16)
            return carry

        lax.fori_loop(0, BAND, fill, 0, unroll=2)

    loads[0].wait()
    band_lane = iota((BAND, LANES), 1)
    band_row = iota((BAND, LANES), 0)

    def band(b):
        return leaf_ref[:, pl.ds(pl.multiple_of(b * BAND, BAND), BAND), :].reshape(deep, cols)

    total = jnp.zeros((records, LANES), F32)
    for b in range(blocks):
        both = jnp.dot(band(b), ends, preferred_element_type=F32).reshape(records, BAND, LANES)
        twice = 2 * (band_row + b * BAND)
        kept = (band_lane == twice) | (band_lane == lax.rem(twice + PC - 1, LANES))
        both = jnp.where(kept[None], both, 0.0).astype(BF16).reshape(deep, LANES)
        total = total + jnp.dot(gather, both, preferred_element_type=F32)
    edge_cols[...] = total.astype(BF16)

    def edge_row(n):
        chosen = gather_last if n % 2 else gather_first
        edge_rows[n] = jnp.dot(chosen, band(n // 2), preferred_element_type=F32).astype(BF16)

    edge_row(0)
    edge_row(2 * blocks - 1)

    pl.semaphore_wait(barrier, len(row_peers) + has_above.astype(jnp.int32) + has_below.astype(jnp.int32))

    def pass_on(k):
        if k:
            @pl.when(a >= k)
            def _():
                pl.semaphore_wait(chain_sem.at[0, k - 1], 1)

            @pl.when(a < n_ax - k)
            def _():
                pl.semaphore_wait(chain_sem.at[1, k - 1], 1)

        if k < n_ax - 1:
            @pl.when((a >= k) & has_above)
            def _():
                pl.semaphore_signal(chain_sem.at[0, k], inc=1, device_id=above, device_id_type=MESH)

            @pl.when((a < n_ax - k) & has_below)
            def _():
                pl.semaphore_signal(chain_sem.at[1, k], inc=1, device_id=below, device_id_type=MESH)

    pass_on(0)

    def halo(src, dst, i, device):
        return pltpu.make_async_remote_copy(
            src_ref=src, dst_ref=dst, send_sem=halo_send.at[i], recv_sem=halo_recv.at[i],
            device_id=device, device_id_type=MESH,
        )

    down = halo(edge_rows.at[2 * blocks - 1], got_rows.at[0], 0, (lax.rem(a + 1, n_ax), z))
    up = halo(edge_rows.at[0], got_rows.at[1], 1, (lax.rem(a + n_ax - 1, n_ax), z))
    right = halo(edge_cols, got_cols.at[0], 2, (a, lax.rem(z + 1, n_az)))
    left = halo(edge_cols, got_cols.at[1], 3, (a, lax.rem(z + n_az - 1, n_az)))

    @pl.when(a < n_ax - 1)
    def _():
        down.start()

    @pl.when(a > 0)
    def _():
        up.start()

    right.start()
    left.start()

    for n in range(1, 2 * blocks - 1):
        edge_row(n)
    held = side // BAND

    def laplace(b):
        def one(c, carry):
            some = pl.ds(pl.multiple_of(c * held, held), held)
            x = leaf_ref[some, b * BAND:(b + 1) * BAND, :].reshape(side, cols)
            total = jnp.dot(x, along, preferred_element_type=F32)
            total = total + jnp.dot(upright, x, preferred_element_type=F32)
            lap_ref[b, pl.ds(pl.multiple_of(c * side, side), side), :] = total.astype(BF16)
            return carry

        lax.fori_loop(0, deep // side, one, 0, unroll=2)

    for b in range(blocks):
        laplace(b)

    def couple(h):
        def one(b, carry):
            found = jnp.dot(law_ref[h], lap_ref[b], preferred_element_type=F32)
            coupled_ref[h, pl.ds(pl.multiple_of(b * BAND, BAND), BAND)] = found.reshape(BAND, wide, cols)
            return carry

        lax.fori_loop(0, blocks, one, 0)
        for b in range(1, blocks):
            add_row(h, b * BAND - 1, edge_rows[2 * b])
            add_row(h, b * BAND, edge_rows[2 * b - 1])

    def add_row(h, r, record_row):
        coupled_ref[h, r] += jnp.dot(small[h], record_row, preferred_element_type=F32)

    near = n_ax - 1 if n_ax & (n_ax - 1) else n_ax // 2
    pass_on(1)
    couple(0)
    for k in range(2, near + 1):
        pass_on(k)

    @pl.when(a > 0)
    def _():
        down.wait_recv()

    @pl.when(a < n_ax - 1)
    def _():
        up.wait_recv()

    right.wait_recv()
    left.wait_recv()
    even = lax.rem(iota((records, LANES), 1), 2) == 0
    beside = jnp.where(even, got_cols[0].astype(F32), got_cols[1].astype(F32)).astype(BF16)

    def border(h):
        side_ref[h] = jnp.dot(small[h], beside, preferred_element_type=F32)
        add_row(h, 0, got_rows[0])
        add_row(h, rows - 1, got_rows[1])

    border(0)

    lane = iota((share, LANES), 1)
    low = lane < PC
    across = cols // PC
    tiles = cols // LANES

    def force(h):
        part = slice(h * share, (h + 1) * share)

        def some(turn, carry):
            stored = []
            for r in [turn * TOGETHER + n for n in range(TOGETHER)]:
                over = pltpu.roll(side_ref[h, :share], lax.rem(2 * LANES - 2 * r, LANES), 1)
                under = pltpu.roll(side_ref[h, share:], lax.rem(2 * LANES + PC - 2 * r, LANES), 1)
                for t in range(tiles):
                    cut = slice(t * LANES, (t + 1) * LANES)
                    top, bottom = coupled_ref[h, r, :share, cut], coupled_ref[h, r, share:, cut]
                    turned = pltpu.roll(jnp.where(low, bottom, top), PC, 1)
                    one, two = jnp.where(low, top, turned), jnp.where(low, turned, bottom)
                    if t == 0:
                        one = one + jnp.where(lane == 0, over, jnp.where(lane == PC, under, 0.0))
                    if t == tiles - 1:
                        two = two + jnp.where(lane == PC - 1, over, jnp.where(lane == LANES - 1, under, 0.0))
                    p = r * across + 2 * t
                    stored.append((p, (fields_ref[p, part] + SPREAD * one).astype(BF16)))
                    stored.append((p + 1, (fields_ref[p + 1, part] + SPREAD * two).astype(BF16)))
            for p, value in stored:
                forced_ref[p, part] = value
            return carry

        lax.fori_loop(0, rows // TOGETHER, some, 0)

    order = shifts(n_ax)
    turns = [n_az - (shift == 0) for shift in order]

    def piece(ref, at, h):
        return ref.at[at] if h is None else ref.at[at, :, h * share:(h + 1) * share]

    def outgoing(j, d, h=None):
        ta, tz = partner(a, order[j], n_ax), lax.rem(z + d + 1, n_az)
        other = ta * n_az + tz
        return other, pltpu.make_async_remote_copy(
            src_ref=piece(packed_ref, other, h), dst_ref=piece(landed_ref, me, h),
            send_sem=send_sem.at[h or 0, j * n_az + d], recv_sem=recv_sem.at[h or 0, j * n_az + d],
            device_id=(ta, tz), device_id_type=MESH,
        )

    def incoming(j, d, h=None):
        source = partner(a, order[j], n_ax, back=True) * n_az + lax.rem(z + n_az - d - 1, n_az)
        return source, pltpu.make_async_remote_copy(
            src_ref=piece(packed_ref, source, h), dst_ref=piece(landed_ref, source, h),
            send_sem=send_sem.at[h or 0, j * n_az + d], recv_sem=recv_sem.at[h or 0, j * n_az + d],
            device_id=(a, z), device_id_type=MESH,
        )

    def send_all(j, h=None):
        part = slice(None) if h is None else slice(h * share, (h + 1) * share)

        def send(d, carry):
            other, copy = outgoing(j, d, h)
            for k in range(each):
                packed_ref[other, k, part] = forced_ref[pick_ref[0, other * each + k], part]
            copy.start()
            return carry

        lax.fori_loop(0, turns[j], send, 0)

    halves = [range(PHASES) if j == 0 else (None,) for j in range(n_ax)]

    loads[3].wait()
    force(0)
    picked.wait()
    send_all(0, 0)
    for k in range(near + 1, n_ax):
        pass_on(k)
    for h in range(1, PHASES):
        couple(h)
        border(h)
        force(h)
        send_all(0, h)
    for j in range(1, n_ax):
        send_all(j)

    for load in loads[4:]:
        load.wait()
    interpolate(coarse_ref, strip_ref)
    row = iota((height, LANES), 0)
    nu = jnp.full((height, LANES), nu_ref[0], F32)
    for f in range(1, FIELDS):
        nu = jnp.where(lax.rem(row, FIELDS) == f, nu_ref[f], nu)

    for k in range(each):
        ghost = strip_ref[slot_ref[me * each + k]]
        block = forced_ref[pick_ref[0, me * each + k]].astype(F32)
        out_ref[me, k] = relax(block, ghost, nu)

    def arrive(j, d):
        for h in halves[j]:
            source, copy = incoming(j, d, h)
            copy.wait_recv()
        for k in range(each):
            ghost = strip_ref[slot_ref[source * each + k]]
            out_ref[source, k] = relax(landed_ref[source, k].astype(F32), ghost, nu)

    far = n_ax // 2
    for j in sorted(range(n_ax), key=lambda j: (order[j] > 0, order[j] != far, order[j] > far, -order[j])):
        def one(d, carry, j=j):
            arrive(j, d)
            return carry

        lax.fori_loop(0, turns[j], one, 0)

    for j in range(n_ax):
        def finish(d, carry, j=j):
            for h in halves[j]:
                outgoing(j, d, h)[1].wait_send()
            return carry

        lax.fori_loop(0, turns[j], finish, 0)

    @pl.when(a < n_ax - 1)
    def _():
        down.wait_send()

    @pl.when(a > 0)
    def _():
        up.wait_send()

    right.wait_send()
    left.wait_send()


def pick_slots(each, owner_ref, pick_row):
    patches = owner_ref.shape[1]
    slots = pick_row.shape[1]
    square = (patches, patches)
    eye = iota(square, 0) == iota(square, 1)
    owner = owner_ref[...]
    across = jnp.broadcast_to(owner, square)
    along = jnp.sum(jnp.where(eye, across, 0), axis=1, keepdims=True)
    earlier = (along == across) & (iota(square, 0) < iota(square, 1))
    rank = jnp.sum(earlier.astype(jnp.int32), axis=0, keepdims=True)
    target = jnp.broadcast_to(owner * each + rank, square)
    target = jnp.sum(jnp.where(eye, target, 0), axis=1, keepdims=True)
    shape = (patches, slots)
    taken = target == iota(shape, 1)
    pick_row[...] = patches + jnp.sum(
        jnp.where(taken, iota(shape, 0) - patches, 0), axis=0, keepdims=True
    )


def interpolate(coarse_ref, strip_ref):
    fine = iota((PC, LANES), 1)
    src = iota((PC, LANES), 0)
    cell = lax.rem(fine, PC)
    near = (fine // PC) * (PC // 2) + cell // 2
    second = jnp.where(
        lax.rem(fine, 2) == 0,
        jnp.where(cell == 0, near, near - 1),
        jnp.where(cell == PC - 1, near, near + 1),
    )
    table = (0.75 * (src == near).astype(F32) + 0.25 * (src == second).astype(F32)).astype(BF16)
    for f in range(FIELDS):
        raw = coarse_ref[:, f * PC:(f + 1) * PC]
        top = raw.astype(BF16)
        rest = (raw - top.astype(F32)).astype(BF16)
        fine_cells = jnp.dot(top, table, preferred_element_type=F32)
        fine_cells = fine_cells + jnp.dot(rest, table, preferred_element_type=F32)
        strip_ref[:, f, :] = fine_cells
        strip_ref[:, FIELDS + f, :] = fine_cells


def relax(state, ghost, nu):
    shape = (8, LANES)
    lane = iota(shape, 1)
    low = iota(shape, 0) < FIELDS
    cell = lax.rem(lane, PC)
    up = (lane < PC) & low
    down = (lane >= PC) & (iota(shape, 0) >= FIELDS)
    count = state.shape[0] // 8
    tiles = [state[8 * j:8 * j + 8] for j in range(count)]
    for _ in range(STEPS):
        swap = [pltpu.roll(t, PC, 1) for t in tiles]
        turned = [ghost] + [pltpu.roll(t, FIELDS, 0) for t in swap] + [ghost]
        fresh = []
        for j, t in enumerate(tiles):
            beyond = jnp.where(up, turned[j], jnp.where(down, turned[j + 2], turned[j + 1]))
            west = jnp.where(cell == 0, 0.0, pltpu.roll(t, 1, 1))
            east = jnp.where(cell == PC - 1, 0.0, pltpu.roll(t, LANES - 1, 1))
            total = swap[j] + beyond + west + east - 4.0 * t
            fresh.append(t + nu[8 * j:8 * j + 8] * total)
        tiles = fresh
    return jnp.concatenate(tiles, axis=0)


def shards(mesh, fields, new_owner, leaflet, stiffness, coarse, coarse_of_slot, viscosity):
    n_ax, n_az = mesh.shape["axial"], mesh.shape["azim"]
    devices = n_ax * n_az
    patches, _, section = fields.shape
    records, rows, cols = leaflet.shape
    each = max(2, 3 * patches // (2 * devices))
    slots = devices * each
    wide = -(-slots // LANES) * LANES
    height = FIELDS * section // LANES
    part = records // PHASES
    view = fields.reshape(patches, FIELDS, section // LANES, LANES).transpose(0, 2, 1, 3)
    view = view.reshape(patches, height, LANES)
    given = (new_owner.reshape(1, patches), coarse_of_slot, viscosity, view, leaflet, stiffness, coarse)
    out = pl.pallas_call(
        functools.partial(send_kernel, n_ax, n_az, each),
        out_shape=pltpu.VMEM((devices, each, height, LANES), F32),
        in_specs=[pl.BlockSpec(memory_space=pltpu.HBM)] * 7,
        out_specs=pl.BlockSpec(memory_space=pltpu.VMEM),
        scratch_shapes=[
            pltpu.VMEM((1, patches), jnp.int32),
            pltpu.SMEM((slots,), jnp.int32),
            pltpu.SMEM((FIELDS,), F32),
            pltpu.VMEM((patches, height, LANES), F32),
            pltpu.VMEM(leaflet.shape, BF16),
            pltpu.VMEM(stiffness.shape, BF16),
            pltpu.VMEM(coarse.shape, F32),
            pltpu.SemaphoreType.DMA((7,)),
            pltpu.VMEM((2 * rows // BAND, records, cols), BF16),
            pltpu.VMEM((records, LANES), BF16),
            pltpu.VMEM((2, records, cols), BF16),
            pltpu.VMEM((2, records, LANES), BF16),
            pltpu.VMEM((rows // BAND, BAND * records, cols), BF16),
            pltpu.VMEM((PHASES, BAND * part, BAND * records), BF16),
            pltpu.VMEM((PHASES, part, LANES), F32),
            pltpu.VMEM((PHASES, rows, part, cols), F32),
            pltpu.VMEM((patches + 1, height, LANES), BF16),
            pltpu.VMEM((devices, each, height, LANES), BF16),
            pltpu.VMEM((devices, each, height, LANES), BF16),
            pltpu.VMEM((coarse.shape[0], 2 * FIELDS, LANES), F32),
            pltpu.VMEM((1, wide), jnp.int32),
            pltpu.SMEM((1, wide), jnp.int32),
            pltpu.SemaphoreType.DMA((4,)),
            pltpu.SemaphoreType.DMA((4,)),
            pltpu.SemaphoreType.DMA((PHASES, devices)),
            pltpu.SemaphoreType.DMA((PHASES, devices)),
            pltpu.SemaphoreType.DMA,
            pltpu.SemaphoreType.REGULAR((2, n_ax - 1)),
        ],
        compiler_params=pltpu.CompilerParams(
            collective_id=0, has_side_effects=True, vmem_limit_bytes=40 << 20
        ),
        name="regrid",
    )(*[pltpu.with_memory_space_constraint(v, pltpu.HBM) for v in given])
    out = out.reshape(slots, section // LANES, FIELDS, LANES).transpose(0, 2, 1, 3)
    return out.reshape(slots, FIELDS, section)


def solution(mesh):
    placed = (
        P(("axial", "azim"), None, None),
        P(("axial", "azim"), None),
        P(None, "axial", "azim"),
        P(),
        P(("axial", "azim"), None),
        P(("axial", "azim")),
        P(),
    )
    return jax.shard_map(
        functools.partial(shards, mesh),
        mesh=mesh,
        in_specs=placed,
        out_specs=P(("axial", "azim"), None, None),
        check_vma=False,
    )
```

```python
import functools
import jax
import jax.numpy as jnp
from jax import lax
from jax.experimental import pallas as pl
from jax.experimental.pallas import tpu as pltpu
from jax.sharding import PartitionSpec as P

PC = 64
FIELDS = 4
STEPS = 2
SPREAD = 0.25
FIRST = 8
BAND = 16
TOGETHER = (8, 4)
LANES = 128
MESH = pl.DeviceIdType.MESH
F32 = jnp.float32
BF16 = jnp.bfloat16


def iota(shape, dim):
    return lax.broadcasted_iota(jnp.int32, shape, dim)


def shifts(n_ax):
    if n_ax & (n_ax - 1):
        away = [n_ax // 2 + ((j + 1) // 2) * (1 - 2 * (j % 2)) for j in range(n_ax)]
        return [d % n_ax for d in away]
    return [k ^ (k >> 1) for k in reversed(range(n_ax))]


def partner(a, shift, n_ax, back=False):
    if n_ax & (n_ax - 1):
        return lax.rem(a + (n_ax - shift if back else shift), n_ax)
    return a ^ shift


def send_kernel(
    n_ax, n_az, each, owner_hbm, slot_hbm, nu_hbm, fields_hbm, leaf_hbm, stiff_hbm, coarse_hbm, out_ref,
    owner_ref, slot_ref, nu_ref, fields_ref, leaf_ref, stiff_ref, coarse_ref, load_sem,
    edge_rows, edge_cols, got_rows, got_cols, lap_ref, law_ref, side_ref, coupled_ref, forced_ref, packed_ref,
    landed_ref, strip_ref, pick_row, pick_ref,
    halo_send, halo_recv, send_sem, recv_sem, pick_sem, chain_sem,
):
    a = lax.axis_index("axial")
    z = lax.axis_index("azim")
    me = a * n_az + z
    devices = n_ax * n_az
    records, rows, cols = leaf_ref.shape
    patches, height, _ = fields_ref.shape
    blocks = rows // BAND
    deep = records * BAND
    pairs = records // FIELDS // 2
    cuts = ((0, FIRST), (FIRST, height - FIRST))

    pairs_in = (
        (leaf_hbm, leaf_ref), (owner_hbm, owner_ref), (stiff_hbm, stiff_ref), (fields_hbm, fields_ref),
        (coarse_hbm, coarse_ref), (slot_hbm, slot_ref), (nu_hbm, nu_ref),
    )
    loads = [
        pltpu.make_async_copy(src, dst, load_sem.at[i]) for i, (src, dst) in enumerate(pairs_in)
    ]
    for load in loads:
        load.start()
    got_rows[...] = jnp.zeros_like(got_rows)
    barrier = pltpu.get_barrier_semaphore()

    row_peers = [(a, lax.rem(z + dz, n_az)) for dz in range(1, n_az)]
    for other in row_peers:
        pl.semaphore_signal(barrier, inc=1, device_id=other, device_id_type=MESH)

    above, below = (a + 1, z), (a - 1, z)
    has_above, has_below = a < n_ax - 1, a > 0

    @pl.when(has_above)
    def _():
        pl.semaphore_signal(barrier, inc=1, device_id=above, device_id_type=MESH)

    @pl.when(has_below)
    def _():
        pl.semaphore_signal(barrier, inc=1, device_id=below, device_id_type=MESH)

    column = iota((records, deep), 1)
    belongs = iota((records, deep), 0) == column // BAND
    gather = belongs.astype(BF16)
    gather_first = (belongs & (lax.rem(column, BAND) == 0)).astype(BF16)
    gather_last = (belongs & (lax.rem(column, BAND) == BAND - 1)).astype(BF16)
    source = iota((cols, LANES), 0)
    odd_lane = lax.rem(iota((cols, LANES), 1), 2) == 1
    ends = (((source == cols - 1) & ~odd_lane) | ((source == 0) & odd_lane)).astype(BF16)

    loads[0].wait()
    band_lane = iota((BAND, LANES), 1)
    band_row = iota((BAND, LANES), 0)

    def band(b):
        return leaf_ref[:, pl.ds(pl.multiple_of(b * BAND, BAND), BAND), :].reshape(deep, cols)

    total = jnp.zeros((records, LANES), F32)
    for b in range(blocks):
        both = jnp.dot(band(b), ends, preferred_element_type=F32).reshape(records, BAND, LANES)
        twice = 2 * (band_row + b * BAND)
        kept = (band_lane == twice) | (band_lane == lax.rem(twice + PC - 1, LANES))
        both = jnp.where(kept[None], both, 0.0).astype(BF16).reshape(deep, LANES)
        total = total + jnp.dot(gather, both, preferred_element_type=F32)
    edge_cols[...] = total.astype(BF16)

    pl.semaphore_wait(barrier, len(row_peers) + has_above.astype(jnp.int32) + has_below.astype(jnp.int32))

    def pass_on(k):
        if k:
            @pl.when(a >= k)
            def _():
                pl.semaphore_wait(chain_sem.at[0, k - 1], 1)

            @pl.when(a < n_ax - k)
            def _():
                pl.semaphore_wait(chain_sem.at[1, k - 1], 1)

        if k < n_ax - 1:
            @pl.when((a >= k) & has_above)
            def _():
                pl.semaphore_signal(chain_sem.at[0, k], inc=1, device_id=above, device_id_type=MESH)

            @pl.when((a < n_ax - k) & has_below)
            def _():
                pl.semaphore_signal(chain_sem.at[1, k], inc=1, device_id=below, device_id_type=MESH)

    pass_on(0)

    def halo(src, dst, i, device):
        return pltpu.make_async_remote_copy(
            src_ref=src, dst_ref=dst, send_sem=halo_send.at[i], recv_sem=halo_recv.at[i],
            device_id=device, device_id_type=MESH,
        )

    down = halo(edge_rows.at[2 * blocks - 1], got_rows.at[0], 0, (lax.rem(a + 1, n_ax), z))
    up = halo(edge_rows.at[0], got_rows.at[1], 1, (lax.rem(a + n_ax - 1, n_ax), z))
    right = halo(edge_cols, got_cols.at[0], 2, (a, lax.rem(z + 1, n_az)))
    left = halo(edge_cols, got_cols.at[1], 3, (a, lax.rem(z + n_az - 1, n_az)))

    right.start()
    left.start()

    def edge_row(n):
        chosen = gather_last if n % 2 else gather_first
        edge_rows[n] = jnp.dot(chosen, band(n // 2), preferred_element_type=F32).astype(BF16)

    edge_row(0)
    edge_row(2 * blocks - 1)

    @pl.when(a < n_ax - 1)
    def _():
        down.start()

    @pl.when(a > 0)
    def _():
        up.start()

    here_col, there_col = iota((cols, cols), 0), iota((cols, cols), 1)
    along = (jnp.abs(here_col - there_col) == 1).astype(F32)
    along = jnp.where(here_col == there_col, -4.0, along).astype(BF16)
    side = 2 * LANES
    here_row, there_row = iota((side, side), 0), iota((side, side), 1)
    upright = (here_row // BAND == there_row // BAND) & (jnp.abs(here_row - there_row) == 1)
    upright = upright.astype(BF16)

    loads[1].wait()
    pick_slots(each, owner_ref, pick_row)
    picked = pltpu.make_async_copy(pick_row, pick_ref, pick_sem)
    picked.start()
    forced_ref[patches] = jnp.zeros(forced_ref.shape[1:], BF16)

    loads[2].wait()
    spread = jnp.dot(stiff_ref[...], gather, preferred_element_type=F32).astype(BF16)
    small = []

    def build(h):
        start, share = cuts[h]
        wide = 2 * share
        row_of = lax.rem(iota((wide, deep), 1), BAND)
        order = iota((wide, records), 0)
        within = lax.rem(order, share)
        wanted = lax.rem(within, FIELDS) * (2 * pairs) + order // share
        wanted = wanted + 2 * (start // FIELDS + within // FIELDS)
        chosen = (iota((wide, records), 1) == wanted).astype(BF16)
        small.append(jnp.dot(chosen, stiff_ref[...], preferred_element_type=F32).astype(BF16))
        base = jnp.dot(chosen, spread, preferred_element_type=F32)

        def fill(r, carry):
            here = pl.ds(pl.multiple_of(2 * BAND * start + r * wide, 16), wide)
            law_ref[here, :] = jnp.where(row_of == r, base, 0.0).astype(BF16)
            return carry

        lax.fori_loop(0, BAND, fill, 0, unroll=2)

    build(0)
    for n in range(1, 2 * blocks - 1):
        edge_row(n)
    held = side // BAND

    def laplace(b):
        def one(c, carry):
            some = pl.ds(pl.multiple_of(c * held, held), held)
            x = leaf_ref[some, b * BAND:(b + 1) * BAND, :].reshape(side, cols)
            total = jnp.dot(x, along, preferred_element_type=F32)
            total = total + jnp.dot(upright, x, preferred_element_type=F32)
            lap_ref[b, pl.ds(pl.multiple_of(c * side, side), side), :] = total.astype(BF16)
            return carry

        lax.fori_loop(0, deep // side, one, 0, unroll=2)

    for b in range(blocks):
        laplace(b)

    def rows_of(h):
        start, share = cuts[h]
        return slice(2 * start, 2 * (start + share))

    def couple(h):
        start, share = cuts[h]

        def one(b, carry):
            law = law_ref[2 * BAND * start:2 * BAND * (start + share), :]
            found = jnp.dot(law, lap_ref[b], preferred_element_type=F32).reshape(BAND, 2 * share, cols)
            coupled_ref[pl.ds(pl.multiple_of(b * BAND, BAND), BAND), rows_of(h), :] = found
            return carry

        lax.fori_loop(0, blocks, one, 0)
        for b in range(1, blocks):
            add_row(h, b * BAND - 1, edge_rows[2 * b])
            add_row(h, b * BAND, edge_rows[2 * b - 1])

    def add_row(h, r, record_row):
        coupled_ref[r, rows_of(h), :] += jnp.dot(small[h], record_row, preferred_element_type=F32)

    near = n_ax - 1 if n_ax & (n_ax - 1) else n_ax // 2
    pass_on(1)
    couple(0)
    for k in range(2, near + 1):
        pass_on(k)

    @pl.when(a > 0)
    def _():
        down.wait_recv()

    @pl.when(a < n_ax - 1)
    def _():
        up.wait_recv()

    right.wait_recv()
    left.wait_recv()
    even = lax.rem(iota((records, LANES), 1), 2) == 0
    beside = jnp.where(even, got_cols[0].astype(F32), got_cols[1].astype(F32)).astype(BF16)

    def border(h):
        side_ref[rows_of(h), :] = jnp.dot(small[h], beside, preferred_element_type=F32)
        add_row(h, 0, got_rows[0])
        add_row(h, rows - 1, got_rows[1])

    border(0)

    across = cols // PC
    tiles = cols // LANES

    def force(h):
        start, share = cuts[h]
        part = slice(start, start + share)
        upper, lower = slice(2 * start, 2 * start + share), slice(2 * start + share, 2 * (start + share))
        lane = iota((share, LANES), 1)
        low = lane < PC
        together = TOGETHER[h]

        def some(turn, carry):
            stored = []
            for r in [turn * together + n for n in range(together)]:
                over = pltpu.roll(side_ref[upper, :], lax.rem(2 * LANES - 2 * r, LANES), 1)
                under = pltpu.roll(side_ref[lower, :], lax.rem(2 * LANES + PC - 2 * r, LANES), 1)
                for t in range(tiles):
                    cut = slice(t * LANES, (t + 1) * LANES)
                    top, bottom = coupled_ref[r, upper, cut], coupled_ref[r, lower, cut]
                    turned = pltpu.roll(jnp.where(low, bottom, top), PC, 1)
                    one, two = jnp.where(low, top, turned), jnp.where(low, turned, bottom)
                    if t == 0:
                        one = one + jnp.where(lane == 0, over, jnp.where(lane == PC, under, 0.0))
                    if t == tiles - 1:
                        two = two + jnp.where(lane == PC - 1, over, jnp.where(lane == LANES - 1, under, 0.0))
                    p = r * across + 2 * t
                    stored.append((p, (fields_ref[p, part] + SPREAD * one).astype(BF16)))
                    stored.append((p + 1, (fields_ref[p + 1, part] + SPREAD * two).astype(BF16)))
            for p, value in stored:
                forced_ref[p, part] = value
            return carry

        lax.fori_loop(0, rows // together, some, 0)

    order = shifts(n_ax)
    turns = [n_az - (shift == 0) for shift in order]

    def piece(ref, at, h):
        return ref.at[at] if h is None else ref.at[at, :, cuts[h][0]:sum(cuts[h])]

    def outgoing(j, d, h=None):
        ta, tz = partner(a, order[j], n_ax), lax.rem(z + d + 1, n_az)
        other = ta * n_az + tz
        return other, pltpu.make_async_remote_copy(
            src_ref=piece(packed_ref, other, h), dst_ref=piece(landed_ref, me, h),
            send_sem=send_sem.at[h or 0, j * n_az + d], recv_sem=recv_sem.at[h or 0, j * n_az + d],
            device_id=(ta, tz), device_id_type=MESH,
        )

    def incoming(j, d, h=None):
        source = partner(a, order[j], n_ax, back=True) * n_az + lax.rem(z + n_az - d - 1, n_az)
        return source, pltpu.make_async_remote_copy(
            src_ref=piece(packed_ref, source, h), dst_ref=piece(landed_ref, source, h),
            send_sem=send_sem.at[h or 0, j * n_az + d], recv_sem=recv_sem.at[h or 0, j * n_az + d],
            device_id=(a, z), device_id_type=MESH,
        )

    def send_all(j, h=None):
        part = slice(None) if h is None else slice(cuts[h][0], sum(cuts[h]))

        def send(d, carry):
            other, copy = outgoing(j, d, h)
            for k in range(each):
                packed_ref[other, k, part] = forced_ref[pick_ref[0, other * each + k], part]
            copy.start()
            return carry

        lax.fori_loop(0, turns[j], send, 0)

    halves = [range(len(cuts)) if j == 0 else (None,) for j in range(n_ax)]

    loads[3].wait()
    force(0)
    picked.wait()
    send_all(0, 0)
    for h in range(1, len(cuts)):
        build(h)
        couple(h)
        border(h)
        force(h)
        send_all(0, h)
    for k in range(near + 1, n_ax):
        pass_on(k)
    for j in range(1, n_ax):
        send_all(j)

    for load in loads[4:]:
        load.wait()
    interpolate(coarse_ref, strip_ref)
    row = iota((height, LANES), 0)
    nu = jnp.full((height, LANES), nu_ref[0], F32)
    for f in range(1, FIELDS):
        nu = jnp.where(lax.rem(row, FIELDS) == f, nu_ref[f], nu)

    for k in range(each):
        ghost = strip_ref[slot_ref[me * each + k]]
        block = forced_ref[pick_ref[0, me * each + k]].astype(F32)
        out_ref[me, k] = relax(block, ghost, nu)

    def arrive(j, d):
        for h in halves[j]:
            source, copy = incoming(j, d, h)
            copy.wait_recv()
        for k in range(each):
            ghost = strip_ref[slot_ref[source * each + k]]
            out_ref[source, k] = relax(landed_ref[source, k].astype(F32), ghost, nu)

    far = n_ax // 2
    for j in sorted(range(n_ax), key=lambda j: (order[j] > 0, order[j] != far, order[j] > far, -order[j])):
        def one(d, carry, j=j):
            arrive(j, d)
            return carry

        lax.fori_loop(0, turns[j], one, 0)

    for j in range(n_ax):
        def finish(d, carry, j=j):
            for h in halves[j]:
                outgoing(j, d, h)[1].wait_send()
            return carry

        lax.fori_loop(0, turns[j], finish, 0)

    @pl.when(a < n_ax - 1)
    def _():
        down.wait_send()

    @pl.when(a > 0)
    def _():
        up.wait_send()

    right.wait_send()
    left.wait_send()


def pick_slots(each, owner_ref, pick_row):
    patches = owner_ref.shape[1]
    slots = pick_row.shape[1]
    square = (patches, patches)
    eye = iota(square, 0) == iota(square, 1)
    owner = owner_ref[...]
    across = jnp.broadcast_to(owner, square)
    along = jnp.sum(jnp.where(eye, across, 0), axis=1, keepdims=True)
    earlier = (along == across) & (iota(square, 0) < iota(square, 1))
    rank = jnp.sum(earlier.astype(jnp.int32), axis=0, keepdims=True)
    target = jnp.broadcast_to(owner * each + rank, square)
    target = jnp.sum(jnp.where(eye, target, 0), axis=1, keepdims=True)
    shape = (patches, slots)
    taken = target == iota(shape, 1)
    pick_row[...] = patches + jnp.sum(
        jnp.where(taken, iota(shape, 0) - patches, 0), axis=0, keepdims=True
    )


def interpolate(coarse_ref, strip_ref):
    fine = iota((PC, LANES), 1)
    src = iota((PC, LANES), 0)
    cell = lax.rem(fine, PC)
    near = (fine // PC) * (PC // 2) + cell // 2
    second = jnp.where(
        lax.rem(fine, 2) == 0,
        jnp.where(cell == 0, near, near - 1),
        jnp.where(cell == PC - 1, near, near + 1),
    )
    table = (0.75 * (src == near).astype(F32) + 0.25 * (src == second).astype(F32)).astype(BF16)
    for f in range(FIELDS):
        raw = coarse_ref[:, f * PC:(f + 1) * PC]
        top = raw.astype(BF16)
        rest = (raw - top.astype(F32)).astype(BF16)
        fine_cells = jnp.dot(top, table, preferred_element_type=F32)
        fine_cells = fine_cells + jnp.dot(rest, table, preferred_element_type=F32)
        strip_ref[:, f, :] = fine_cells
        strip_ref[:, FIELDS + f, :] = fine_cells


def relax(state, ghost, nu):
    shape = (8, LANES)
    lane = iota(shape, 1)
    low = iota(shape, 0) < FIELDS
    cell = lax.rem(lane, PC)
    up = (lane < PC) & low
    down = (lane >= PC) & (iota(shape, 0) >= FIELDS)
    count = state.shape[0] // 8
    tiles = [state[8 * j:8 * j + 8] for j in range(count)]
    for _ in range(STEPS):
        swap = [pltpu.roll(t, PC, 1) for t in tiles]
        turned = [ghost] + [pltpu.roll(t, FIELDS, 0) for t in swap] + [ghost]
        fresh = []
        for j, t in enumerate(tiles):
            beyond = jnp.where(up, turned[j], jnp.where(down, turned[j + 2], turned[j + 1]))
            west = jnp.where(cell == 0, 0.0, pltpu.roll(t, 1, 1))
            east = jnp.where(cell == PC - 1, 0.0, pltpu.roll(t, LANES - 1, 1))
            total = swap[j] + beyond + west + east - 4.0 * t
            fresh.append(t + nu[8 * j:8 * j + 8] * total)
        tiles = fresh
    return jnp.concatenate(tiles, axis=0)


def shards(mesh, fields, new_owner, leaflet, stiffness, coarse, coarse_of_slot, viscosity):
    n_ax, n_az = mesh.shape["axial"], mesh.shape["azim"]
    devices = n_ax * n_az
    patches, _, section = fields.shape
    records, rows, cols = leaflet.shape
    each = max(2, 3 * patches // (2 * devices))
    slots = devices * each
    wide = -(-slots // LANES) * LANES
    height = FIELDS * section // LANES
    view = fields.reshape(patches, FIELDS, section // LANES, LANES).transpose(0, 2, 1, 3)
    view = view.reshape(patches, height, LANES)
    given = (new_owner.reshape(1, patches), coarse_of_slot, viscosity, view, leaflet, stiffness, coarse)
    out = pl.pallas_call(
        functools.partial(send_kernel, n_ax, n_az, each),
        out_shape=pltpu.VMEM((devices, each, height, LANES), F32),
        in_specs=[pl.BlockSpec(memory_space=pltpu.HBM)] * 7,
        out_specs=pl.BlockSpec(memory_space=pltpu.VMEM),
        scratch_shapes=[
            pltpu.VMEM((1, patches), jnp.int32),
            pltpu.SMEM((slots,), jnp.int32),
            pltpu.SMEM((FIELDS,), F32),
            pltpu.VMEM((patches, height, LANES), F32),
            pltpu.VMEM(leaflet.shape, BF16),
            pltpu.VMEM(stiffness.shape, BF16),
            pltpu.VMEM(coarse.shape, F32),
            pltpu.SemaphoreType.DMA((7,)),
            pltpu.VMEM((2 * rows // BAND, records, cols), BF16),
            pltpu.VMEM((records, LANES), BF16),
            pltpu.VMEM((2, records, cols), BF16),
            pltpu.VMEM((2, records, LANES), BF16),
            pltpu.VMEM((rows // BAND, BAND * records, cols), BF16),
            pltpu.VMEM((BAND * records, BAND * records), BF16),
            pltpu.VMEM((records, LANES), F32),
            pltpu.VMEM((rows, records, cols), F32),
            pltpu.VMEM((patches + 1, height, LANES), BF16),
            pltpu.VMEM((devices, each, height, LANES), BF16),
            pltpu.VMEM((devices, each, height, LANES), BF16),
            pltpu.VMEM((coarse.shape[0], 2 * FIELDS, LANES), F32),
            pltpu.VMEM((1, wide), jnp.int32),
            pltpu.SMEM((1, wide), jnp.int32),
            pltpu.SemaphoreType.DMA((4,)),
            pltpu.SemaphoreType.DMA((4,)),
            pltpu.SemaphoreType.DMA((2, devices)),
            pltpu.SemaphoreType.DMA((2, devices)),
            pltpu.SemaphoreType.DMA,
            pltpu.SemaphoreType.REGULAR((2, n_ax - 1)),
        ],
        compiler_params=pltpu.CompilerParams(
            collective_id=0, has_side_effects=True, vmem_limit_bytes=40 << 20
        ),
        name="regrid",
    )(*[pltpu.with_memory_space_constraint(v, pltpu.HBM) for v in given])
    out = out.reshape(slots, section // LANES, FIELDS, LANES).transpose(0, 2, 1, 3)
    return out.reshape(slots, FIELDS, section)


def solution(mesh):
    placed = (
        P(("axial", "azim"), None, None),
        P(("axial", "azim"), None),
        P(None, "axial", "azim"),
        P(),
        P(("axial", "azim"), None),
        P(("axial", "azim")),
        P(),
    )
    return jax.shard_map(
        functools.partial(shards, mesh),
        mesh=mesh,
        in_specs=placed,
        out_specs=P(("axial", "azim"), None, None),
        check_vma=False,
    )
```

```python
import functools
import jax
import jax.numpy as jnp
from jax import lax
from jax.experimental import pallas as pl
from jax.experimental.pallas import tpu as pltpu
from jax.sharding import PartitionSpec as P

PC = 64
FIELDS = 4
STEPS = 2
SPREAD = 0.25
FIRST = 8
BAND = 16
TOGETHER = (8, 4)
LANES = 128
MESH = pl.DeviceIdType.MESH
F32 = jnp.float32
BF16 = jnp.bfloat16


def iota(shape, dim):
    return lax.broadcasted_iota(jnp.int32, shape, dim)


def shifts(n_ax):
    if n_ax & (n_ax - 1):
        away = [n_ax // 2 + ((j + 1) // 2) * (1 - 2 * (j % 2)) for j in range(n_ax)]
        return [d % n_ax for d in away]
    return [k ^ (k >> 1) for k in reversed(range(n_ax))]


def partner(a, shift, n_ax, back=False):
    if n_ax & (n_ax - 1):
        return lax.rem(a + (n_ax - shift if back else shift), n_ax)
    return a ^ shift


def send_kernel(
    n_ax, n_az, each, owner_hbm, slot_hbm, nu_hbm, fields_hbm, leaf_hbm, stiff_hbm, coarse_hbm, out_ref,
    owner_ref, slot_ref, nu_ref, fields_ref, leaf_ref, stiff_ref, coarse_ref, load_sem,
    edge_rows, edge_cols, got_rows, got_cols, lap_ref, law_ref, side_ref, coupled_ref, forced_ref, packed_ref,
    landed_ref, strip_ref, pick_row, pick_ref,
    halo_send, halo_recv, send_sem, recv_sem, pick_sem, chain_sem,
):
    a = lax.axis_index("axial")
    z = lax.axis_index("azim")
    me = a * n_az + z
    devices = n_ax * n_az
    records, rows, cols = leaf_ref.shape
    patches, height, _ = fields_ref.shape
    blocks = rows // BAND
    deep = records * BAND
    pairs = records // FIELDS // 2
    cuts = ((0, FIRST), (FIRST, height - FIRST))

    pairs_in = (
        (leaf_hbm, leaf_ref), (owner_hbm, owner_ref), (stiff_hbm, stiff_ref), (fields_hbm, fields_ref),
        (coarse_hbm, coarse_ref), (slot_hbm, slot_ref), (nu_hbm, nu_ref),
    )
    loads = [
        pltpu.make_async_copy(src, dst, load_sem.at[i]) for i, (src, dst) in enumerate(pairs_in)
    ]
    for load in loads:
        load.start()
    got_rows[...] = jnp.zeros_like(got_rows)
    barrier = pltpu.get_barrier_semaphore()

    row_peers = [(a, lax.rem(z + dz, n_az)) for dz in range(1, n_az)]
    for other in row_peers:
        pl.semaphore_signal(barrier, inc=1, device_id=other, device_id_type=MESH)

    above, below = (a + 1, z), (a - 1, z)
    has_above, has_below = a < n_ax - 1, a > 0

    @pl.when(has_above)
    def _():
        pl.semaphore_signal(barrier, inc=1, device_id=above, device_id_type=MESH)

    @pl.when(has_below)
    def _():
        pl.semaphore_signal(barrier, inc=1, device_id=below, device_id_type=MESH)

    column = iota((records, deep), 1)
    belongs = iota((records, deep), 0) == column // BAND
    gather = belongs.astype(BF16)
    gather_first = (belongs & (lax.rem(column, BAND) == 0)).astype(BF16)
    gather_last = (belongs & (lax.rem(column, BAND) == BAND - 1)).astype(BF16)
    source = iota((cols, LANES), 0)
    odd_lane = lax.rem(iota((cols, LANES), 1), 2) == 1
    ends = (((source == cols - 1) & ~odd_lane) | ((source == 0) & odd_lane)).astype(BF16)

    loads[0].wait()
    band_lane = iota((BAND, LANES), 1)
    band_row = iota((BAND, LANES), 0)

    def band(b):
        return leaf_ref[:, pl.ds(pl.multiple_of(b * BAND, BAND), BAND), :].reshape(deep, cols)

    total = jnp.zeros((records, LANES), F32)
    for b in range(blocks):
        both = jnp.dot(band(b), ends, preferred_element_type=F32).reshape(records, BAND, LANES)
        twice = 2 * (band_row + b * BAND)
        kept = (band_lane == twice) | (band_lane == lax.rem(twice + PC - 1, LANES))
        both = jnp.where(kept[None], both, 0.0).astype(BF16).reshape(deep, LANES)
        total = total + jnp.dot(gather, both, preferred_element_type=F32)
    edge_cols[...] = total.astype(BF16)

    pl.semaphore_wait(barrier, len(row_peers) + has_above.astype(jnp.int32) + has_below.astype(jnp.int32))

    def pass_on(k):
        if k:
            @pl.when(a >= k)
            def _():
                pl.semaphore_wait(chain_sem.at[0, k - 1], 1)

            @pl.when(a < n_ax - k)
            def _():
                pl.semaphore_wait(chain_sem.at[1, k - 1], 1)

        if k < n_ax - 1:
            @pl.when((a >= k) & has_above)
            def _():
                pl.semaphore_signal(chain_sem.at[0, k], inc=1, device_id=above, device_id_type=MESH)

            @pl.when((a < n_ax - k) & has_below)
            def _():
                pl.semaphore_signal(chain_sem.at[1, k], inc=1, device_id=below, device_id_type=MESH)

    pass_on(0)

    def halo(src, dst, i, device):
        return pltpu.make_async_remote_copy(
            src_ref=src, dst_ref=dst, send_sem=halo_send.at[i], recv_sem=halo_recv.at[i],
            device_id=device, device_id_type=MESH,
        )

    down = halo(edge_rows.at[2 * blocks - 1], got_rows.at[0], 0, (lax.rem(a + 1, n_ax), z))
    up = halo(edge_rows.at[0], got_rows.at[1], 1, (lax.rem(a + n_ax - 1, n_ax), z))
    right = halo(edge_cols, got_cols.at[0], 2, (a, lax.rem(z + 1, n_az)))
    left = halo(edge_cols, got_cols.at[1], 3, (a, lax.rem(z + n_az - 1, n_az)))

    right.start()
    left.start()

    def edge_row(n):
        chosen = gather_last if n % 2 else gather_first
        edge_rows[n] = jnp.dot(chosen, band(n // 2), preferred_element_type=F32).astype(BF16)

    edge_row(0)
    edge_row(2 * blocks - 1)

    @pl.when(a < n_ax - 1)
    def _():
        down.start()

    @pl.when(a > 0)
    def _():
        up.start()

    here_col, there_col = iota((cols, cols), 0), iota((cols, cols), 1)
    along = (jnp.abs(here_col - there_col) == 1).astype(F32)
    along = jnp.where(here_col == there_col, -4.0, along).astype(BF16)
    side = 2 * LANES
    here_row, there_row = iota((side, side), 0), iota((side, side), 1)
    upright = (here_row // BAND == there_row // BAND) & (jnp.abs(here_row - there_row) == 1)
    upright = upright.astype(BF16)

    loads[1].wait()
    pick_slots(each, owner_ref, pick_row)
    picked = pltpu.make_async_copy(pick_row, pick_ref, pick_sem)
    picked.start()
    forced_ref[patches] = jnp.zeros(forced_ref.shape[1:], BF16)

    loads[2].wait()
    spread = jnp.dot(stiff_ref[...], gather, preferred_element_type=F32).astype(BF16)
    small = []

    def build(h):
        start, share = cuts[h]
        wide = 2 * share
        row_of = lax.rem(iota((wide, deep), 1), BAND)
        order = iota((wide, records), 0)
        within = lax.rem(order, share)
        wanted = lax.rem(within, FIELDS) * (2 * pairs) + order // share
        wanted = wanted + 2 * (start // FIELDS + within // FIELDS)
        chosen = (iota((wide, records), 1) == wanted).astype(BF16)
        small.append(jnp.dot(chosen, stiff_ref[...], preferred_element_type=F32).astype(BF16))
        base = jnp.dot(chosen, spread, preferred_element_type=F32)

        def fill(r, carry):
            here = pl.ds(pl.multiple_of(2 * BAND * start + r * wide, 16), wide)
            law_ref[here, :] = jnp.where(row_of == r, base, 0.0).astype(BF16)
            return carry

        lax.fori_loop(0, BAND, fill, 0, unroll=2)

    build(0)
    for n in range(1, 2 * blocks - 1):
        edge_row(n)
    held = side // BAND

    def laplace(b):
        def one(c, carry):
            some = pl.ds(pl.multiple_of(c * held, held), held)
            x = leaf_ref[some, b * BAND:(b + 1) * BAND, :].reshape(side, cols)
            total = jnp.dot(x, along, preferred_element_type=F32)
            total = total + jnp.dot(upright, x, preferred_element_type=F32)
            lap_ref[b, pl.ds(pl.multiple_of(c * side, side), side), :] = total.astype(BF16)
            return carry

        lax.fori_loop(0, deep // side, one, 0, unroll=2)

    for b in range(blocks):
        laplace(b)

    def rows_of(h):
        start, share = cuts[h]
        return slice(2 * start, 2 * (start + share))

    def couple(h):
        start, share = cuts[h]

        def one(b, carry):
            law = law_ref[2 * BAND * start:2 * BAND * (start + share), :]
            found = jnp.dot(law, lap_ref[b], preferred_element_type=F32).reshape(BAND, 2 * share, cols)
            coupled_ref[pl.ds(pl.multiple_of(b * BAND, BAND), BAND), rows_of(h), :] = found
            return carry

        lax.fori_loop(0, blocks, one, 0)
        for b in range(1, blocks):
            add_row(h, b * BAND - 1, edge_rows[2 * b])
            add_row(h, b * BAND, edge_rows[2 * b - 1])

    def add_row(h, r, record_row):
        coupled_ref[r, rows_of(h), :] += jnp.dot(small[h], record_row, preferred_element_type=F32)

    near = n_ax - 1 if n_ax & (n_ax - 1) else n_ax // 2
    pass_on(1)
    couple(0)
    for k in range(2, near + 1):
        pass_on(k)

    @pl.when(a > 0)
    def _():
        down.wait_recv()

    @pl.when(a < n_ax - 1)
    def _():
        up.wait_recv()

    right.wait_recv()
    left.wait_recv()
    even = lax.rem(iota((records, LANES), 1), 2) == 0
    beside = jnp.where(even, got_cols[0].astype(F32), got_cols[1].astype(F32)).astype(BF16)

    def border(h):
        side_ref[rows_of(h), :] = jnp.dot(small[h], beside, preferred_element_type=F32)
        add_row(h, 0, got_rows[0])
        add_row(h, rows - 1, got_rows[1])

    border(0)

    across = cols // PC
    tiles = cols // LANES

    def force(h):
        start, share = cuts[h]
        part = slice(start, start + share)
        upper, lower = slice(2 * start, 2 * start + share), slice(2 * start + share, 2 * (start + share))
        lane = iota((share, LANES), 1)
        low = lane < PC
        together = TOGETHER[h]

        def some(turn, carry):
            stored = []
            for r in [turn * together + n for n in range(together)]:
                over = pltpu.roll(side_ref[upper, :], lax.rem(2 * LANES - 2 * r, LANES), 1)
                under = pltpu.roll(side_ref[lower, :], lax.rem(2 * LANES + PC - 2 * r, LANES), 1)
                for t in range(tiles):
                    cut = slice(t * LANES, (t + 1) * LANES)
                    top, bottom = coupled_ref[r, upper, cut], coupled_ref[r, lower, cut]
                    turned = pltpu.roll(jnp.where(low, bottom, top), PC, 1)
                    one, two = jnp.where(low, top, turned), jnp.where(low, turned, bottom)
                    if t == 0:
                        one = one + jnp.where(lane == 0, over, jnp.where(lane == PC, under, 0.0))
                    if t == tiles - 1:
                        two = two + jnp.where(lane == PC - 1, over, jnp.where(lane == LANES - 1, under, 0.0))
                    p = r * across + 2 * t
                    stored.append((p, (fields_ref[p, part] + SPREAD * one).astype(BF16)))
                    stored.append((p + 1, (fields_ref[p + 1, part] + SPREAD * two).astype(BF16)))
            for p, value in stored:
                forced_ref[p, part] = value
            return carry

        lax.fori_loop(0, rows // together, some, 0)

    order = shifts(n_ax)
    turns = [n_az - (shift == 0) for shift in order]

    def piece(ref, at, h):
        return ref.at[at] if h is None else ref.at[at, :, cuts[h][0]:sum(cuts[h])]

    def outgoing(j, d, h=None):
        ta, tz = partner(a, order[j], n_ax), lax.rem(z + d + 1, n_az)
        other = ta * n_az + tz
        return other, pltpu.make_async_remote_copy(
            src_ref=piece(packed_ref, other, h), dst_ref=piece(landed_ref, me, h),
            send_sem=send_sem.at[h or 0, j * n_az + d], recv_sem=recv_sem.at[h or 0, j * n_az + d],
            device_id=(ta, tz), device_id_type=MESH,
        )

    def incoming(j, d, h=None):
        source = partner(a, order[j], n_ax, back=True) * n_az + lax.rem(z + n_az - d - 1, n_az)
        return source, pltpu.make_async_remote_copy(
            src_ref=piece(packed_ref, source, h), dst_ref=piece(landed_ref, source, h),
            send_sem=send_sem.at[h or 0, j * n_az + d], recv_sem=recv_sem.at[h or 0, j * n_az + d],
            device_id=(a, z), device_id_type=MESH,
        )

    def send_all(j, h=None):
        part = slice(None) if h is None else slice(cuts[h][0], sum(cuts[h]))

        def send(d, carry):
            other, copy = outgoing(j, d, h)
            for k in range(each):
                packed_ref[other, k, part] = forced_ref[pick_ref[0, other * each + k], part]
            copy.start()
            return carry

        lax.fori_loop(0, turns[j], send, 0)

    halves = [range(len(cuts)) if j == 0 else (None,) for j in range(n_ax)]

    loads[3].wait()
    force(0)
    picked.wait()
    send_all(0, 0)
    for h in range(1, len(cuts)):
        build(h)
        couple(h)
        border(h)
        force(h)
        send_all(0, h)
    for k in range(near + 1, n_ax):
        pass_on(k)
    for j in range(1, n_ax):
        send_all(j)

    @pl.when(a < n_ax - 1)
    def _():
        down.wait_send()

    @pl.when(a > 0)
    def _():
        up.wait_send()

    right.wait_send()
    left.wait_send()

    for load in loads[4:]:
        load.wait()
    interpolate(coarse_ref, strip_ref)
    row = iota((height, LANES), 0)
    nu = jnp.full((height, LANES), nu_ref[0], F32)
    for f in range(1, FIELDS):
        nu = jnp.where(lax.rem(row, FIELDS) == f, nu_ref[f], nu)

    for k in range(each):
        ghost = strip_ref[slot_ref[me * each + k]]
        block = forced_ref[pick_ref[0, me * each + k]].astype(F32)
        out_ref[me, k] = relax(block, ghost, nu)

    def arrive(j, d):
        for h in halves[j]:
            source, copy = incoming(j, d, h)
            copy.wait_recv()
        for k in range(each):
            ghost = strip_ref[slot_ref[source * each + k]]
            out_ref[source, k] = relax(landed_ref[source, k].astype(F32), ghost, nu)

    def finish(j):
        def one(d, carry):
            for h in halves[j]:
                outgoing(j, d, h)[1].wait_send()
            return carry

        lax.fori_loop(0, turns[j], one, 0)

    far = n_ax // 2
    visits = sorted(range(n_ax), key=lambda j: (order[j] > 0, order[j] != far, order[j] > far, -order[j]))
    for j in visits:
        if j == visits[-1]:
            for other in visits[:-1]:
                finish(other)

        def one(d, carry, j=j):
            arrive(j, d)
            return carry

        lax.fori_loop(0, turns[j], one, 0)

    finish(visits[-1])


def pick_slots(each, owner_ref, pick_row):
    patches = owner_ref.shape[1]
    slots = pick_row.shape[1]
    square = (patches, patches)
    eye = iota(square, 0) == iota(square, 1)
    owner = owner_ref[...]
    across = jnp.broadcast_to(owner, square)
    along = jnp.sum(jnp.where(eye, across, 0), axis=1, keepdims=True)
    earlier = (along == across) & (iota(square, 0) < iota(square, 1))
    rank = jnp.sum(earlier.astype(jnp.int32), axis=0, keepdims=True)
    target = jnp.broadcast_to(owner * each + rank, square)
    target = jnp.sum(jnp.where(eye, target, 0), axis=1, keepdims=True)
    shape = (patches, slots)
    taken = target == iota(shape, 1)
    pick_row[...] = patches + jnp.sum(
        jnp.where(taken, iota(shape, 0) - patches, 0), axis=0, keepdims=True
    )


def interpolate(coarse_ref, strip_ref):
    fine = iota((PC, LANES), 1)
    src = iota((PC, LANES), 0)
    cell = lax.rem(fine, PC)
    near = (fine // PC) * (PC // 2) + cell // 2
    second = jnp.where(
        lax.rem(fine, 2) == 0,
        jnp.where(cell == 0, near, near - 1),
        jnp.where(cell == PC - 1, near, near + 1),
    )
    table = (0.75 * (src == near).astype(F32) + 0.25 * (src == second).astype(F32)).astype(BF16)
    for f in range(FIELDS):
        raw = coarse_ref[:, f * PC:(f + 1) * PC]
        top = raw.astype(BF16)
        rest = (raw - top.astype(F32)).astype(BF16)
        fine_cells = jnp.dot(top, table, preferred_element_type=F32)
        fine_cells = fine_cells + jnp.dot(rest, table, preferred_element_type=F32)
        strip_ref[:, f, :] = fine_cells
        strip_ref[:, FIELDS + f, :] = fine_cells


def relax(state, ghost, nu):
    shape = (8, LANES)
    lane = iota(shape, 1)
    low = iota(shape, 0) < FIELDS
    cell = lax.rem(lane, PC)
    up = (lane < PC) & low
    down = (lane >= PC) & (iota(shape, 0) >= FIELDS)
    count = state.shape[0] // 8
    tiles = [state[8 * j:8 * j + 8] for j in range(count)]
    for _ in range(STEPS):
        swap = [pltpu.roll(t, PC, 1) for t in tiles]
        turned = [ghost] + [pltpu.roll(t, FIELDS, 0) for t in swap] + [ghost]
        fresh = []
        for j, t in enumerate(tiles):
            beyond = jnp.where(up, turned[j], jnp.where(down, turned[j + 2], turned[j + 1]))
            west = jnp.where(cell == 0, 0.0, pltpu.roll(t, 1, 1))
            east = jnp.where(cell == PC - 1, 0.0, pltpu.roll(t, LANES - 1, 1))
            total = swap[j] + beyond + west + east - 4.0 * t
            fresh.append(t + nu[8 * j:8 * j + 8] * total)
        tiles = fresh
    return jnp.concatenate(tiles, axis=0)


def shards(mesh, fields, new_owner, leaflet, stiffness, coarse, coarse_of_slot, viscosity):
    n_ax, n_az = mesh.shape["axial"], mesh.shape["azim"]
    devices = n_ax * n_az
    patches, _, section = fields.shape
    records, rows, cols = leaflet.shape
    each = max(2, 3 * patches // (2 * devices))
    slots = devices * each
    wide = -(-slots // LANES) * LANES
    height = FIELDS * section // LANES
    view = fields.reshape(patches, FIELDS, section // LANES, LANES).transpose(0, 2, 1, 3)
    view = view.reshape(patches, height, LANES)
    given = (new_owner.reshape(1, patches), coarse_of_slot, viscosity, view, leaflet, stiffness, coarse)
    out = pl.pallas_call(
        functools.partial(send_kernel, n_ax, n_az, each),
        out_shape=pltpu.VMEM((devices, each, height, LANES), F32),
        in_specs=[pl.BlockSpec(memory_space=pltpu.HBM)] * 7,
        out_specs=pl.BlockSpec(memory_space=pltpu.VMEM),
        scratch_shapes=[
            pltpu.VMEM((1, patches), jnp.int32),
            pltpu.SMEM((slots,), jnp.int32),
            pltpu.SMEM((FIELDS,), F32),
            pltpu.VMEM((patches, height, LANES), F32),
            pltpu.VMEM(leaflet.shape, BF16),
            pltpu.VMEM(stiffness.shape, BF16),
            pltpu.VMEM(coarse.shape, F32),
            pltpu.SemaphoreType.DMA((7,)),
            pltpu.VMEM((2 * rows // BAND, records, cols), BF16),
            pltpu.VMEM((records, LANES), BF16),
            pltpu.VMEM((2, records, cols), BF16),
            pltpu.VMEM((2, records, LANES), BF16),
            pltpu.VMEM((rows // BAND, BAND * records, cols), BF16),
            pltpu.VMEM((BAND * records, BAND * records), BF16),
            pltpu.VMEM((records, LANES), F32),
            pltpu.VMEM((rows, records, cols), F32),
            pltpu.VMEM((patches + 1, height, LANES), BF16),
            pltpu.VMEM((devices, each, height, LANES), BF16),
            pltpu.VMEM((devices, each, height, LANES), BF16),
            pltpu.VMEM((coarse.shape[0], 2 * FIELDS, LANES), F32),
            pltpu.VMEM((1, wide), jnp.int32),
            pltpu.SMEM((1, wide), jnp.int32),
            pltpu.SemaphoreType.DMA((4,)),
            pltpu.SemaphoreType.DMA((4,)),
            pltpu.SemaphoreType.DMA((2, devices)),
            pltpu.SemaphoreType.DMA((2, devices)),
            pltpu.SemaphoreType.DMA,
            pltpu.SemaphoreType.REGULAR((2, n_ax - 1)),
        ],
        compiler_params=pltpu.CompilerParams(
            collective_id=0, has_side_effects=True, vmem_limit_bytes=40 << 20
        ),
        name="regrid",
    )(*[pltpu.with_memory_space_constraint(v, pltpu.HBM) for v in given])
    out = out.reshape(slots, section // LANES, FIELDS, LANES).transpose(0, 2, 1, 3)
    return out.reshape(slots, FIELDS, section)


def solution(mesh):
    placed = (
        P(("axial", "azim"), None, None),
        P(("axial", "azim"), None),
        P(None, "axial", "azim"),
        P(),
        P(("axial", "azim"), None),
        P(("axial", "azim")),
        P(),
    )
    return jax.shard_map(
        functools.partial(shards, mesh),
        mesh=mesh,
        in_specs=placed,
        out_specs=P(("axial", "azim"), None, None),
        check_vma=False,
    )
```

```python
import functools
import jax
import jax.numpy as jnp
from jax import lax
from jax.experimental import pallas as pl
from jax.experimental.pallas import tpu as pltpu
from jax.sharding import PartitionSpec as P

PC = 64
FIELDS = 4
STEPS = 2
SPREAD = 0.25
FIRST = 8
BAND = 16
TOGETHER = (8, 4)
LANES = 128
MESH = pl.DeviceIdType.MESH
F32 = jnp.float32
BF16 = jnp.bfloat16


def iota(shape, dim):
    return lax.broadcasted_iota(jnp.int32, shape, dim)


def shifts(n_ax):
    if n_ax & (n_ax - 1):
        away = [n_ax // 2 + ((j + 1) // 2) * (1 - 2 * (j % 2)) for j in range(n_ax)]
        return [d % n_ax for d in away]
    return [k ^ (k >> 1) for k in reversed(range(n_ax))]


def partner(a, shift, n_ax, back=False):
    if n_ax & (n_ax - 1):
        return lax.rem(a + (n_ax - shift if back else shift), n_ax)
    return a ^ shift


def send_kernel(
    n_ax, n_az, each, owner_hbm, slot_hbm, nu_hbm, fields_hbm, leaf_hbm, stiff_hbm, coarse_hbm, out_ref,
    owner_ref, slot_ref, nu_ref, fields_ref, leaf_ref, stiff_ref, coarse_ref, load_sem,
    edge_rows, edge_cols, got_rows, got_cols, lap_ref, law_ref, side_ref, coupled_ref, forced_ref, packed_ref,
    landed_ref, strip_ref, pick_row, pick_ref,
    halo_send, halo_recv, send_sem, recv_sem, pick_sem, chain_sem,
):
    a = lax.axis_index("axial")
    z = lax.axis_index("azim")
    me = a * n_az + z
    devices = n_ax * n_az
    records, rows, cols = leaf_ref.shape
    patches, height, _ = fields_ref.shape
    blocks = rows // BAND
    deep = records * BAND
    pairs = records // FIELDS // 2
    cuts = ((0, FIRST), (FIRST, height - FIRST))

    pairs_in = (
        (leaf_hbm, leaf_ref), (owner_hbm, owner_ref), (stiff_hbm, stiff_ref), (fields_hbm, fields_ref),
        (coarse_hbm, coarse_ref), (slot_hbm, slot_ref), (nu_hbm, nu_ref),
    )
    loads = [
        pltpu.make_async_copy(src, dst, load_sem.at[i]) for i, (src, dst) in enumerate(pairs_in)
    ]
    for load in loads:
        load.start()
    got_rows[...] = jnp.zeros_like(got_rows)
    barrier = pltpu.get_barrier_semaphore()

    row_peers = [(a, lax.rem(z + dz, n_az)) for dz in range(1, n_az)]
    for other in row_peers:
        pl.semaphore_signal(barrier, inc=1, device_id=other, device_id_type=MESH)

    above, below = (a + 1, z), (a - 1, z)
    has_above, has_below = a < n_ax - 1, a > 0

    @pl.when(has_above)
    def _():
        pl.semaphore_signal(barrier, inc=1, device_id=above, device_id_type=MESH)

    @pl.when(has_below)
    def _():
        pl.semaphore_signal(barrier, inc=1, device_id=below, device_id_type=MESH)

    column = iota((records, deep), 1)
    belongs = iota((records, deep), 0) == column // BAND
    gather = belongs.astype(BF16)
    gather_first = (belongs & (lax.rem(column, BAND) == 0)).astype(BF16)
    gather_last = (belongs & (lax.rem(column, BAND) == BAND - 1)).astype(BF16)
    source = iota((cols, LANES), 0)
    odd_lane = lax.rem(iota((cols, LANES), 1), 2) == 1
    ends = (((source == cols - 1) & ~odd_lane) | ((source == 0) & odd_lane)).astype(BF16)

    here_col, there_col = iota((cols, cols), 0), iota((cols, cols), 1)
    along = (jnp.abs(here_col - there_col) == 1).astype(F32)
    along = jnp.where(here_col == there_col, -4.0, along).astype(BF16)
    side = 2 * LANES
    here_row, there_row = iota((side, side), 0), iota((side, side), 1)
    upright = (here_row // BAND == there_row // BAND) & (jnp.abs(here_row - there_row) == 1)
    upright = upright.astype(BF16)

    loads[2].wait()
    spread = jnp.dot(stiff_ref[...], gather, preferred_element_type=F32).astype(BF16)
    small = []

    def build(h):
        start, share = cuts[h]
        wide = 2 * share
        row_of = lax.rem(iota((wide, deep), 1), BAND)
        order = iota((wide, records), 0)
        within = lax.rem(order, share)
        wanted = lax.rem(within, FIELDS) * (2 * pairs) + order // share
        wanted = wanted + 2 * (start // FIELDS + within // FIELDS)
        chosen = (iota((wide, records), 1) == wanted).astype(BF16)
        small.append(jnp.dot(chosen, stiff_ref[...], preferred_element_type=F32).astype(BF16))
        base = jnp.dot(chosen, spread, preferred_element_type=F32)

        def fill(r, carry):
            here = pl.ds(pl.multiple_of(2 * BAND * start + r * wide, 16), wide)
            law_ref[here, :] = jnp.where(row_of == r, base, 0.0).astype(BF16)
            return carry

        lax.fori_loop(0, BAND, fill, 0, unroll=2)

    build(0)
    loads[0].wait()
    band_lane = iota((BAND, LANES), 1)
    band_row = iota((BAND, LANES), 0)

    def band(b):
        return leaf_ref[:, pl.ds(pl.multiple_of(b * BAND, BAND), BAND), :].reshape(deep, cols)

    total = jnp.zeros((records, LANES), F32)
    for b in range(blocks):
        both = jnp.dot(band(b), ends, preferred_element_type=F32).reshape(records, BAND, LANES)
        twice = 2 * (band_row + b * BAND)
        kept = (band_lane == twice) | (band_lane == lax.rem(twice + PC - 1, LANES))
        both = jnp.where(kept[None], both, 0.0).astype(BF16).reshape(deep, LANES)
        total = total + jnp.dot(gather, both, preferred_element_type=F32)
    edge_cols[...] = total.astype(BF16)

    pl.semaphore_wait(barrier, len(row_peers) + has_above.astype(jnp.int32) + has_below.astype(jnp.int32))

    def pass_on(k):
        if k:
            @pl.when(a >= k)
            def _():
                pl.semaphore_wait(chain_sem.at[0, k - 1], 1)

            @pl.when(a < n_ax - k)
            def _():
                pl.semaphore_wait(chain_sem.at[1, k - 1], 1)

        if k < n_ax - 1:
            @pl.when((a >= k) & has_above)
            def _():
                pl.semaphore_signal(chain_sem.at[0, k], inc=1, device_id=above, device_id_type=MESH)

            @pl.when((a < n_ax - k) & has_below)
            def _():
                pl.semaphore_signal(chain_sem.at[1, k], inc=1, device_id=below, device_id_type=MESH)

    pass_on(0)

    def halo(src, dst, i, device):
        return pltpu.make_async_remote_copy(
            src_ref=src, dst_ref=dst, send_sem=halo_send.at[i], recv_sem=halo_recv.at[i],
            device_id=device, device_id_type=MESH,
        )

    down = halo(edge_rows.at[2 * blocks - 1], got_rows.at[0], 0, (lax.rem(a + 1, n_ax), z))
    up = halo(edge_rows.at[0], got_rows.at[1], 1, (lax.rem(a + n_ax - 1, n_ax), z))
    right = halo(edge_cols, got_cols.at[0], 2, (a, lax.rem(z + 1, n_az)))
    left = halo(edge_cols, got_cols.at[1], 3, (a, lax.rem(z + n_az - 1, n_az)))

    right.start()
    left.start()

    def edge_row(n):
        chosen = gather_last if n % 2 else gather_first
        edge_rows[n] = jnp.dot(chosen, band(n // 2), preferred_element_type=F32).astype(BF16)

    edge_row(0)
    edge_row(2 * blocks - 1)

    @pl.when(a < n_ax - 1)
    def _():
        down.start()

    @pl.when(a > 0)
    def _():
        up.start()

    loads[1].wait()
    pick_slots(each, owner_ref, pick_row)
    picked = pltpu.make_async_copy(pick_row, pick_ref, pick_sem)
    picked.start()
    forced_ref[patches] = jnp.zeros(forced_ref.shape[1:], BF16)

    for n in range(1, 2 * blocks - 1):
        edge_row(n)
    held = side // BAND

    def laplace(b):
        def one(c, carry):
            some = pl.ds(pl.multiple_of(c * held, held), held)
            x = leaf_ref[some, b * BAND:(b + 1) * BAND, :].reshape(side, cols)
            total = jnp.dot(x, along, preferred_element_type=F32)
            total = total + jnp.dot(upright, x, preferred_element_type=F32)
            lap_ref[b, pl.ds(pl.multiple_of(c * side, side), side), :] = total.astype(BF16)
            return carry

        lax.fori_loop(0, deep // side, one, 0, unroll=2)

    for b in range(blocks):
        laplace(b)

    def rows_of(h):
        start, share = cuts[h]
        return slice(2 * start, 2 * (start + share))

    def couple(h):
        start, share = cuts[h]

        def one(b, carry):
            law = law_ref[2 * BAND * start:2 * BAND * (start + share), :]
            found = jnp.dot(law, lap_ref[b], preferred_element_type=F32).reshape(BAND, 2 * share, cols)
            coupled_ref[pl.ds(pl.multiple_of(b * BAND, BAND), BAND), rows_of(h), :] = found
            return carry

        lax.fori_loop(0, blocks, one, 0)
        for b in range(1, blocks):
            add_row(h, b * BAND - 1, edge_rows[2 * b])
            add_row(h, b * BAND, edge_rows[2 * b - 1])

    def add_row(h, r, record_row):
        coupled_ref[r, rows_of(h), :] += jnp.dot(small[h], record_row, preferred_element_type=F32)

    near = n_ax - 1 if n_ax & (n_ax - 1) else n_ax // 2
    pass_on(1)
    couple(0)
    for k in range(2, near + 1):
        pass_on(k)

    @pl.when(a > 0)
    def _():
        down.wait_recv()

    @pl.when(a < n_ax - 1)
    def _():
        up.wait_recv()

    right.wait_recv()
    left.wait_recv()
    even = lax.rem(iota((records, LANES), 1), 2) == 0
    beside = jnp.where(even, got_cols[0].astype(F32), got_cols[1].astype(F32)).astype(BF16)

    def border(h):
        side_ref[rows_of(h), :] = jnp.dot(small[h], beside, preferred_element_type=F32)
        add_row(h, 0, got_rows[0])
        add_row(h, rows - 1, got_rows[1])

    border(0)

    across = cols // PC
    tiles = cols // LANES

    def force(h):
        start, share = cuts[h]
        part = slice(start, start + share)
        upper, lower = slice(2 * start, 2 * start + share), slice(2 * start + share, 2 * (start + share))
        lane = iota((share, LANES), 1)
        low = lane < PC
        together = TOGETHER[h]

        def some(turn, carry):
            stored = []
            for r in [turn * together + n for n in range(together)]:
                over = pltpu.roll(side_ref[upper, :], lax.rem(2 * LANES - 2 * r, LANES), 1)
                under = pltpu.roll(side_ref[lower, :], lax.rem(2 * LANES + PC - 2 * r, LANES), 1)
                for t in range(tiles):
                    cut = slice(t * LANES, (t + 1) * LANES)
                    top, bottom = coupled_ref[r, upper, cut], coupled_ref[r, lower, cut]
                    turned = pltpu.roll(jnp.where(low, bottom, top), PC, 1)
                    one, two = jnp.where(low, top, turned), jnp.where(low, turned, bottom)
                    if t == 0:
                        one = one + jnp.where(lane == 0, over, jnp.where(lane == PC, under, 0.0))
                    if t == tiles - 1:
                        two = two + jnp.where(lane == PC - 1, over, jnp.where(lane == LANES - 1, under, 0.0))
                    p = r * across + 2 * t
                    stored.append((p, (fields_ref[p, part] + SPREAD * one).astype(BF16)))
                    stored.append((p + 1, (fields_ref[p + 1, part] + SPREAD * two).astype(BF16)))
            for p, value in stored:
                forced_ref[p, part] = value
            return carry

        lax.fori_loop(0, rows // together, some, 0)

    order = shifts(n_ax)
    turns = [n_az - (shift == 0) for shift in order]

    def piece(ref, at, h):
        return ref.at[at] if h is None else ref.at[at, :, cuts[h][0]:sum(cuts[h])]

    def outgoing(j, d, h=None):
        ta, tz = partner(a, order[j], n_ax), lax.rem(z + d + 1, n_az)
        other = ta * n_az + tz
        return other, pltpu.make_async_remote_copy(
            src_ref=piece(packed_ref, other, h), dst_ref=piece(landed_ref, me, h),
            send_sem=send_sem.at[h or 0, j * n_az + d], recv_sem=recv_sem.at[h or 0, j * n_az + d],
            device_id=(ta, tz), device_id_type=MESH,
        )

    def incoming(j, d, h=None):
        source = partner(a, order[j], n_ax, back=True) * n_az + lax.rem(z + n_az - d - 1, n_az)
        return source, pltpu.make_async_remote_copy(
            src_ref=piece(packed_ref, source, h), dst_ref=piece(landed_ref, source, h),
            send_sem=send_sem.at[h or 0, j * n_az + d], recv_sem=recv_sem.at[h or 0, j * n_az + d],
            device_id=(a, z), device_id_type=MESH,
        )

    def send_all(j, h=None):
        part = slice(None) if h is None else slice(cuts[h][0], sum(cuts[h]))

        def send(d, carry):
            other, copy = outgoing(j, d, h)
            for k in range(each):
                packed_ref[other, k, part] = forced_ref[pick_ref[0, other * each + k], part]
            copy.start()
            return carry

        lax.fori_loop(0, turns[j], send, 0)

    halves = [range(len(cuts)) if j == 0 else (None,) for j in range(n_ax)]

    loads[3].wait()
    force(0)
    picked.wait()
    send_all(0, 0)
    for h in range(1, len(cuts)):
        build(h)
        couple(h)
        border(h)
        force(h)
        send_all(0, h)
    for k in range(near + 1, n_ax):
        pass_on(k)
    for j in range(1, n_ax):
        send_all(j)

    @pl.when(a < n_ax - 1)
    def _():
        down.wait_send()

    @pl.when(a > 0)
    def _():
        up.wait_send()

    right.wait_send()
    left.wait_send()

    for load in loads[4:]:
        load.wait()
    interpolate(coarse_ref, strip_ref)
    row = iota((height, LANES), 0)
    nu = jnp.full((height, LANES), nu_ref[0], F32)
    for f in range(1, FIELDS):
        nu = jnp.where(lax.rem(row, FIELDS) == f, nu_ref[f], nu)

    for k in range(each):
        ghost = strip_ref[slot_ref[me * each + k]]
        block = forced_ref[pick_ref[0, me * each + k]].astype(F32)
        out_ref[me, k] = relax(block, ghost, nu)

    def arrive(j, d):
        for h in halves[j]:
            source, copy = incoming(j, d, h)
            copy.wait_recv()
        for k in range(each):
            ghost = strip_ref[slot_ref[source * each + k]]
            out_ref[source, k] = relax(landed_ref[source, k].astype(F32), ghost, nu)

    def finish(j):
        def one(d, carry):
            for h in halves[j]:
                outgoing(j, d, h)[1].wait_send()
            return carry

        lax.fori_loop(0, turns[j], one, 0)

    far = n_ax // 2
    visits = sorted(range(n_ax), key=lambda j: (order[j] > 0, order[j] != far, order[j] > far, -order[j]))
    for j in visits:
        if j == visits[-1]:
            for other in visits[:-1]:
                finish(other)

        def one(d, carry, j=j):
            arrive(j, d)
            return carry

        lax.fori_loop(0, turns[j], one, 0)

    finish(visits[-1])


def pick_slots(each, owner_ref, pick_row):
    patches = owner_ref.shape[1]
    slots = pick_row.shape[1]
    square = (patches, patches)
    eye = iota(square, 0) == iota(square, 1)
    owner = owner_ref[...]
    across = jnp.broadcast_to(owner, square)
    along = jnp.sum(jnp.where(eye, across, 0), axis=1, keepdims=True)
    earlier = (along == across) & (iota(square, 0) < iota(square, 1))
    rank = jnp.sum(earlier.astype(jnp.int32), axis=0, keepdims=True)
    target = jnp.broadcast_to(owner * each + rank, square)
    target = jnp.sum(jnp.where(eye, target, 0), axis=1, keepdims=True)
    shape = (patches, slots)
    taken = target == iota(shape, 1)
    pick_row[...] = patches + jnp.sum(
        jnp.where(taken, iota(shape, 0) - patches, 0), axis=0, keepdims=True
    )


def interpolate(coarse_ref, strip_ref):
    fine = iota((PC, LANES), 1)
    src = iota((PC, LANES), 0)
    cell = lax.rem(fine, PC)
    near = (fine // PC) * (PC // 2) + cell // 2
    second = jnp.where(
        lax.rem(fine, 2) == 0,
        jnp.where(cell == 0, near, near - 1),
        jnp.where(cell == PC - 1, near, near + 1),
    )
    table = (0.75 * (src == near).astype(F32) + 0.25 * (src == second).astype(F32)).astype(BF16)
    for f in range(FIELDS):
        raw = coarse_ref[:, f * PC:(f + 1) * PC]
        top = raw.astype(BF16)
        rest = (raw - top.astype(F32)).astype(BF16)
        fine_cells = jnp.dot(top, table, preferred_element_type=F32)
        fine_cells = fine_cells + jnp.dot(rest, table, preferred_element_type=F32)
        strip_ref[:, f, :] = fine_cells
        strip_ref[:, FIELDS + f, :] = fine_cells


def relax(state, ghost, nu):
    shape = (8, LANES)
    lane = iota(shape, 1)
    low = iota(shape, 0) < FIELDS
    cell = lax.rem(lane, PC)
    up = (lane < PC) & low
    down = (lane >= PC) & (iota(shape, 0) >= FIELDS)
    count = state.shape[0] // 8
    tiles = [state[8 * j:8 * j + 8] for j in range(count)]
    for _ in range(STEPS):
        swap = [pltpu.roll(t, PC, 1) for t in tiles]
        turned = [ghost] + [pltpu.roll(t, FIELDS, 0) for t in swap] + [ghost]
        fresh = []
        for j, t in enumerate(tiles):
            beyond = jnp.where(up, turned[j], jnp.where(down, turned[j + 2], turned[j + 1]))
            west = jnp.where(cell == 0, 0.0, pltpu.roll(t, 1, 1))
            east = jnp.where(cell == PC - 1, 0.0, pltpu.roll(t, LANES - 1, 1))
            total = swap[j] + beyond + west + east - 4.0 * t
            fresh.append(t + nu[8 * j:8 * j + 8] * total)
        tiles = fresh
    return jnp.concatenate(tiles, axis=0)


def shards(mesh, fields, new_owner, leaflet, stiffness, coarse, coarse_of_slot, viscosity):
    n_ax, n_az = mesh.shape["axial"], mesh.shape["azim"]
    devices = n_ax * n_az
    patches, _, section = fields.shape
    records, rows, cols = leaflet.shape
    each = max(2, 3 * patches // (2 * devices))
    slots = devices * each
    wide = -(-slots // LANES) * LANES
    height = FIELDS * section // LANES
    view = fields.reshape(patches, FIELDS, section // LANES, LANES).transpose(0, 2, 1, 3)
    view = view.reshape(patches, height, LANES)
    given = (new_owner.reshape(1, patches), coarse_of_slot, viscosity, view, leaflet, stiffness, coarse)
    out = pl.pallas_call(
        functools.partial(send_kernel, n_ax, n_az, each),
        out_shape=pltpu.VMEM((devices, each, height, LANES), F32),
        in_specs=[pl.BlockSpec(memory_space=pltpu.HBM)] * 7,
        out_specs=pl.BlockSpec(memory_space=pltpu.VMEM),
        scratch_shapes=[
            pltpu.VMEM((1, patches), jnp.int32),
            pltpu.SMEM((slots,), jnp.int32),
            pltpu.SMEM((FIELDS,), F32),
            pltpu.VMEM((patches, height, LANES), F32),
            pltpu.VMEM(leaflet.shape, BF16),
            pltpu.VMEM(stiffness.shape, BF16),
            pltpu.VMEM(coarse.shape, F32),
            pltpu.SemaphoreType.DMA((7,)),
            pltpu.VMEM((2 * rows // BAND, records, cols), BF16),
            pltpu.VMEM((records, LANES), BF16),
            pltpu.VMEM((2, records, cols), BF16),
            pltpu.VMEM((2, records, LANES), BF16),
            pltpu.VMEM((rows // BAND, BAND * records, cols), BF16),
            pltpu.VMEM((BAND * records, BAND * records), BF16),
            pltpu.VMEM((records, LANES), F32),
            pltpu.VMEM((rows, records, cols), F32),
            pltpu.VMEM((patches + 1, height, LANES), BF16),
            pltpu.VMEM((devices, each, height, LANES), BF16),
            pltpu.VMEM((devices, each, height, LANES), BF16),
            pltpu.VMEM((coarse.shape[0], 2 * FIELDS, LANES), F32),
            pltpu.VMEM((1, wide), jnp.int32),
            pltpu.SMEM((1, wide), jnp.int32),
            pltpu.SemaphoreType.DMA((4,)),
            pltpu.SemaphoreType.DMA((4,)),
            pltpu.SemaphoreType.DMA((2, devices)),
            pltpu.SemaphoreType.DMA((2, devices)),
            pltpu.SemaphoreType.DMA,
            pltpu.SemaphoreType.REGULAR((2, n_ax - 1)),
        ],
        compiler_params=pltpu.CompilerParams(
            collective_id=0, has_side_effects=True, vmem_limit_bytes=40 << 20
        ),
        name="regrid",
    )(*[pltpu.with_memory_space_constraint(v, pltpu.HBM) for v in given])
    out = out.reshape(slots, section // LANES, FIELDS, LANES).transpose(0, 2, 1, 3)
    return out.reshape(slots, FIELDS, section)


def solution(mesh):
    placed = (
        P(("axial", "azim"), None, None),
        P(("axial", "azim"), None),
        P(None, "axial", "azim"),
        P(),
        P(("axial", "azim"), None),
        P(("axial", "azim")),
        P(),
    )
    return jax.shard_map(
        functools.partial(shards, mesh),
        mesh=mesh,
        in_specs=placed,
        out_specs=P(("axial", "azim"), None, None),
        check_vma=False,
    )
```
